512 devices in a mesh: wide: 64 (over y, z_lo, core), narrow: 8 (over x, z_hi).
Axes of the slice: x: 4, y: 4, z: 16 (z_hi: 2, z_lo: 8; z = z_hi * 8 + z_lo), core: 2. Of those that a mesh axis runs over, the one named last changes fastest.
Arguments:
- lifted_field: bfloat16 [64, 32, 64, 128], P('wide', None, 'narrow'), may hold values from -6 to 6
- spectral_weight: float32 [256, 16, 2, 32, 32], P('wide', 'narrow'), may hold values from -0.75 to 0.75
- mix_weight: bfloat16 [32, 32], replicated, may hold values from -1 to 1
- mix_bias: float32 [32], replicated, may hold values from -3 to 3
- head_weight: bfloat16 [32, 128], replicated, may hold values from -1 to 1
- head_bias: float32 [128], replicated, may hold values from -3 to 3
- out_weight: bfloat16 [128], replicated, may hold values from -0.5 to 0.5
- cotangent: float32 [64, 64, 128], P('wide', 'narrow'), may hold values from -6 to 6
Outputs:
- prediction: float32 [64, 64, 128], P('wide', 'narrow')
- grad_field: bfloat16 [64, 32, 64, 128], P('wide', None, 'narrow')
- grad_spectral: float32 [256, 16, 2, 32, 32], P('wide', 'narrow')
- grad_mix: float32 [32, 32], replicated
- grad_head: float32 [32, 128], replicated
The draws below stay inside these ranges and needn't reach their ends.
All inputs are finite; a program needn't handle non-finite values.
Results may differ from the reference program's by a relative error of at most 0.018.
Values may be sent and summed in bfloat16 or wider, within the bound.
A program may use at most 64 MiB of HBM per device.

```python
import math
import jax
import jax.numpy as jnp
from jax import lax

C = 32
HID = 128
MX = 16
MY = 16
MZ = 16
NZ = 128
NX = 64
NY = 64


def plane_wave(number_key, offset_key, wave_count, length, lowest, highest):
    number = jax.random.randint(number_key, (wave_count, C, 1), lowest, highest, dtype=jnp.int32)
    positions = jnp.arange(length, dtype=jnp.int32)[None, None, :]
    turned = jnp.mod(number * positions, length).astype(jnp.float32) * (2.0 * math.pi / length)
    offsets = jax.random.uniform(offset_key, (wave_count, C, 1), jnp.float32, -math.pi, math.pi)
    return jnp.cos(turned + offsets)


def draw_lifted_field(base_key, part):
    subkeys = jax.random.split(base_key, 8)
    wave_count = 6
    rough_part = 0.8 * jnp.clip(jax.random.normal(subkeys[0], (NX, C, NY, NZ), jnp.float32), -4.0, 4.0)
    amplitude = jax.random.uniform(subkeys[1], (wave_count, C), jnp.float32, -0.4, 0.4)
    along_x = plane_wave(subkeys[2], subkeys[5], wave_count, NX, -7, 8)
    along_y = plane_wave(subkeys[3], subkeys[6], wave_count, NY, -7, 8)
    along_z = plane_wave(subkeys[4], subkeys[7], wave_count, NZ, 0, 16)
    summed = rough_part
    for wave_index in range(wave_count):
        x_part = jnp.transpose(along_x[wave_index])[:, :, None, None]
        y_part = (amplitude[wave_index][:, None] * along_y[wave_index])[None, :, :, None]
        z_part = along_z[wave_index][None, :, None, :]
        summed = summed + x_part * y_part * z_part
    return summed.astype(jnp.bfloat16)


def level_of(own_key, dims, shards, smallest, largest):
    factor_of, own = 1.0, jax.random.fold_in(own_key, 6)
    for position, parts in shards:
        steps = jnp.exp(jax.random.uniform(jax.random.fold_in(own, position), (parts,), jnp.float32, smallest / len(shards), largest / len(shards)))
        factor_of = factor_of * jnp.repeat(steps, dims[position] // parts).reshape([-1 if axis == position else 1 for axis in range(len(dims))])
    return factor_of


def noise(own_key, extent, spread, limit, cuts=(), held_as=jnp.bfloat16):
    values = jax.random.normal(own_key, extent, jnp.float32) * spread
    if len(cuts) > 0:
        values = level_of(own_key, extent, cuts, -0.22, 0.18) * values
    return jnp.clip(values, min=-limit, max=limit).astype(held_as)


def setup_inputs(seed: int = 0) -> dict:
    key_list = jax.random.split(jax.random.key(seed), 9)
    lifted_field = draw_lifted_field(jax.random.fold_in(key_list[8], 71), 0)
    spectral_weight = noise(key_list[1], (MX * MY, MZ, 2, C, C), (2 * C) ** -0.5, 0.75, ((0, 64), (1, 8)), jnp.float32)
    mix_weight = noise(key_list[2], (C, C), C ** -0.5, 1.0)
    mix_bias = noise(key_list[3], (C,), 0.5, 3.0, (), jnp.float32)
    head_weight = noise(key_list[4], (C, HID), C ** -0.5, 1.0)
    head_bias = noise(key_list[5], (HID,), 0.5, 3.0, (), jnp.float32)
    out_weight = noise(key_list[6], (HID,), HID ** -0.5, 0.5)
    cotangent = noise(key_list[7], (NX, NY, NZ), 1.0, 6.0, ((0, 64), (1, 8)), jnp.float32)
    return {"lifted_field": lifted_field, "spectral_weight": spectral_weight, "mix_weight": mix_weight, "mix_bias": mix_bias, "head_weight": head_weight, "head_bias": head_bias, "out_weight": out_weight, "cotangent": cotangent}


HIGHEST_PRECISION = lax.Precision.HIGHEST

def round_half(values):
    return lax.optimization_barrier(values.astype(jnp.bfloat16)).astype(jnp.float32)

def signed_freq(indices, kept_count):
    return jnp.where(indices < kept_count // 2, indices, indices - kept_count)

def phases(positions, frequency, length):
    turned = jnp.mod(positions[:, None] * frequency[None, :], length)
    return turned.astype(jnp.float32) * (2.0 * math.pi / length)

def real_forward(positions, length, kept_count, doubled):
    indices = jnp.arange(kept_count, dtype=jnp.int32)
    angles = phases(positions, indices, length)
    if doubled:
        scaling = 1.0 + (indices > 0).astype(jnp.float32)
    else:
        scaling = jnp.ones((kept_count,), jnp.float32)
    scaling = scaling * (1.0 / math.sqrt(length))
    return jnp.stack([jnp.cos(angles) * scaling, -jnp.sin(angles) * scaling], axis=1)

def real_inverse(positions, length, kept_count, doubled):
    return jnp.transpose(real_forward(positions, length, kept_count, doubled), (2, 1, 0))

def complex_forward(positions, frequency, length):
    angles = phases(positions, frequency, length)
    cosine = jnp.cos(angles) * (1.0 / math.sqrt(length))
    sine = jnp.sin(angles) * (1.0 / math.sqrt(length))
    return jnp.stack([jnp.stack([cosine, sine]), jnp.stack([-sine, cosine])])

def complex_inverse(positions, frequency, length):
    angles = phases(positions, frequency, length)
    cosine = jnp.transpose(jnp.cos(angles)) * (1.0 / math.sqrt(length))
    sine = jnp.transpose(jnp.sin(angles)) * (1.0 / math.sqrt(length))
    return jnp.stack([jnp.stack([cosine, -sine]), jnp.stack([sine, cosine])])

def activation(values):
    return jax.nn.gelu(values, approximate=False)

def activation_slope(values):
    cumulative = 0.5 * (1.0 + lax.erf(values * (1.0 / math.sqrt(2.0))))
    return cumulative + values * jnp.exp(-0.5 * values * values) * (1.0 / math.sqrt(2.0 * math.pi))

def mode_forward(spectrum, weights):
    real_part = spectrum[:, :, 0]
    imag_part = spectrum[:, :, 1]
    real_weight = weights[:, :, 0]
    imag_weight = weights[:, :, 1]

    def combine(spectrum_part, weight_part):
        return jnp.einsum('mki,mkio->mko', spectrum_part, weight_part, precision=HIGHEST_PRECISION)
    out_real = combine(real_part, real_weight) - combine(imag_part, imag_weight)
    out_imag = combine(imag_part, real_weight) + combine(real_part, imag_weight)
    return jnp.stack([out_real, out_imag], axis=2)

def mode_backward(spectrum, weights, gradient):
    real_part = spectrum[:, :, 0]
    imag_part = spectrum[:, :, 1]
    real_weight = weights[:, :, 0]
    imag_weight = weights[:, :, 1]
    real_grad = gradient[:, :, 0]
    imag_grad = gradient[:, :, 1]

    def pulled(weight_part, grad_part):
        return jnp.einsum('mkio,mko->mki', weight_part, grad_part, precision=HIGHEST_PRECISION)

    def product(spectrum_part, grad_part):
        return jnp.einsum('mki,mko->mkio', spectrum_part, grad_part, precision=HIGHEST_PRECISION)
    back_real = pulled(real_weight, real_grad) + pulled(imag_weight, imag_grad)
    back_imag = pulled(real_weight, imag_grad) - pulled(imag_weight, real_grad)
    weight_real = product(real_part, real_grad) + product(imag_part, imag_grad)
    weight_imag = product(real_part, imag_grad) - product(imag_part, real_grad)
    return (jnp.stack([back_real, back_imag], axis=2), jnp.stack([weight_real, weight_imag], axis=2))

def analysis(values, doubled):
    z_table = round_half(real_forward(jnp.arange(NZ, dtype=jnp.int32), NZ, MZ, doubled))
    y_table = round_half(complex_forward(jnp.arange(NY, dtype=jnp.int32), signed_freq(jnp.arange(MY, dtype=jnp.int32), MY), NY))
    x_table = complex_forward(jnp.arange(NX, dtype=jnp.int32), signed_freq(jnp.arange(MX, dtype=jnp.int32), MX), NX)

    def one_row(field_row):
        return jnp.einsum('cyz,zrk->krcy', field_row.astype(jnp.float32), z_table, precision=HIGHEST_PRECISION).astype(jnp.bfloat16)
    row_spectra = lax.map(one_row, values)
    planes = jnp.einsum('xkrcn,srnj->kscxj', row_spectra.astype(jnp.float32), y_table, precision=HIGHEST_PRECISION)
    spectrum = jnp.einsum('kscxj,tsxi->ijktc', planes, x_table, precision=HIGHEST_PRECISION)
    return spectrum.reshape(MX * MY, MZ, 2, C)

def synthesis(spectrum, doubled):
    z_table = round_half(real_inverse(jnp.arange(NZ, dtype=jnp.int32), NZ, MZ, doubled))
    y_table = round_half(complex_inverse(jnp.arange(NY, dtype=jnp.int32), signed_freq(jnp.arange(MY, dtype=jnp.int32), MY), NY))
    x_table = round_half(complex_inverse(jnp.arange(NX, dtype=jnp.int32), signed_freq(jnp.arange(MX, dtype=jnp.int32), MX), NX))
    grid_modes = spectrum.astype(jnp.float32).reshape(MX, MY, MZ, 2, C)
    planes = round_half(jnp.einsum('ijkrc,srix->kscxj', grid_modes, x_table, precision=HIGHEST_PRECISION))
    line_data = round_half(jnp.einsum('krcxj,srjn->xkscn', planes, y_table, precision=HIGHEST_PRECISION))
    return (line_data, z_table)

def reference(lifted_field, spectral_weight, mix_weight, mix_bias, head_weight, head_bias, out_weight, cotangent):
    mix_float = mix_weight.astype(jnp.float32)
    head_float = head_weight.astype(jnp.float32)
    out_float = out_weight.astype(jnp.float32)

    def branch_of(line_row, z_table):
        return jnp.einsum('krcn,krz->cnz', line_row, z_table, precision=HIGHEST_PRECISION)
    spectrum = analysis(lifted_field, False)
    lines_fwd, forward_z = synthesis(mode_forward(spectrum, spectral_weight).astype(jnp.bfloat16), True)

    def head_rows(row_items):
        field_row, line_row, target_row = row_items
        field_float = field_row.astype(jnp.float32)
        mixed = jnp.einsum('cyz,cd->dyz', field_float, mix_float, precision=HIGHEST_PRECISION)
        pre_act = branch_of(line_row, forward_z) + mixed + mix_bias[:, None, None]
        hidden = activation(pre_act).astype(jnp.bfloat16).astype(jnp.float32)
        head_pre = jnp.einsum('cyz,cj->jyz', hidden, head_float, precision=HIGHEST_PRECISION) + head_bias[:, None, None]
        active = round_half(activation(head_pre))
        predicted = jnp.einsum('jyz,j->yz', active, out_float, precision=HIGHEST_PRECISION)
        head_slope = round_half(target_row[None] * out_float[:, None, None] * activation_slope(head_pre))
        returned = jnp.einsum('jyz,cj->cyz', head_slope, head_float, precision=HIGHEST_PRECISION)
        grad_row = (returned * activation_slope(pre_act)).astype(jnp.bfloat16)
        head_grad = jnp.einsum('cyz,jyz->cj', hidden, head_slope, precision=HIGHEST_PRECISION)
        mix_grad = jnp.einsum('cyz,dyz->cd', field_float, grad_row.astype(jnp.float32), precision=HIGHEST_PRECISION)
        return (predicted, grad_row, head_grad, mix_grad)
    prediction, grad_pre, head_parts, mix_parts = lax.map(head_rows, (lifted_field, lines_fwd, cotangent))
    adjoint = analysis(grad_pre, True)
    back_modes, grad_spectral = mode_backward(spectrum, spectral_weight, adjoint)
    lines_back, adjoint_z = synthesis(back_modes.astype(jnp.bfloat16), False)

    def back_rows(row_items):
        back_row, grad_row = row_items
        through = branch_of(back_row, adjoint_z) + jnp.einsum('dyz,cd->cyz', grad_row.astype(jnp.float32), mix_float, precision=HIGHEST_PRECISION)
        return through.astype(jnp.bfloat16)
    grad_field = lax.map(back_rows, (lines_back, grad_pre))
    grad_mix = lax.optimization_barrier(jnp.sum(mix_parts, axis=0))
    grad_head = lax.optimization_barrier(jnp.sum(head_parts, axis=0))
    return (prediction, grad_field, grad_spectral, grad_mix, grad_head)
```

```python
import functools
import math

import jax
import jax.numpy as jnp
import ml_dtypes
import numpy as np
from jax import lax
from jax.experimental import pallas as pl
from jax.experimental.pallas import tpu as pltpu
from jax.sharding import PartitionSpec as P

MESH = pl.DeviceIdType.MESH
BF = jnp.bfloat16
F32 = jnp.float32
NX, NY, NZ, C, HID = 64, 64, 128, 32, 128
CROSS = [(dx, dy, dc) for dx in range(4) for dy in range(4) for dc in range(2) if dx or dy or dc]
CROSS.sort(key=lambda t: (-(min(t[0], 4 - t[0]) + min(t[1], 4 - t[1])), t))
RING = sorted(range(1, 16), key=lambda d: (-min(d, 16 - d), d))


def angle(position, frequency, length):
    return 2.0 * math.pi * ((position * frequency) % length) / length


def narrow_type(table):
    return np.asarray(table, np.float32).astype(ml_dtypes.bfloat16)


@functools.lru_cache(None)
def z_tables():
    forward = np.zeros((2, 2, 4, 2, 4, NZ))
    inverse = np.zeros((2, 2, 4, 2, 4, NZ))
    z = np.arange(NZ)
    for flag in range(2):
        for k in range(16):
            scale = (2.0 if flag and k else 1.0) / math.sqrt(NZ)
            real, imag = scale * np.cos(angle(z, k, NZ)), -scale * np.sin(angle(z, k, NZ))
            x, kk = k // 4, k % 4
            forward[flag, 0, x, 0, kk], forward[flag, 0, x, 1, kk] = real, imag
            forward[flag, 1, x, 0, kk], forward[flag, 1, x, 1, kk] = imag, -real
            inverse[flag, 0, x, 0, kk], inverse[flag, 0, x, 1, kk] = real, imag
            inverse[flag, 1, x, 0, kk], inverse[flag, 1, x, 1, kk] = imag, -real
    return narrow_type(forward.reshape(2, 64, NZ)), narrow_type(inverse.reshape(2, 64, NZ))


def frequency(i):
    return i if i < 8 else i - 16


@functools.lru_cache(None)
def y_tables():
    out = np.zeros((8, 2, 8, 16, C), np.float32)
    for n in range(8):
        for y in range(8):
            for place in range(16):
                core, par, low = place // 8, (place // 4) % 2, place % 4
                theta = angle(8 * n + y, frequency((2 * par + core) * 4 + low), NY)
                out[n, 0, y, place] = math.cos(theta) / 8.0
                out[n, 1, y, place] = math.sin(theta) / 8.0
    return out.reshape(8, 16, 512)


@functools.lru_cache(None)
def x_tables():
    forward = np.zeros((4, 8, 16, 2, 2, 4, 2, 2, 2, 4), np.float32)
    inverse = np.zeros((4, 8, 16, 2, 2, 4, 2, 2, 2, 4), np.float32)
    for y in range(4):
        for zl in range(8):
            for i4 in range(4):
                for y2 in range(4):
                    for c2 in range(2):
                        theta = angle(16 * y2 + 2 * zl + c2, frequency(4 * y + i4), NX)
                        co, si = math.cos(theta) / 8.0, math.sin(theta) / 8.0
                        for par in range(2):
                            for zh in range(2):
                                for k2 in range(2):
                                    z2, kk = zh * 8 + 2 * i4 + par, 2 * zh + k2
                                    for s, t, value in ((0, 0, co), (0, 1, si), (1, 0, -si), (1, 1, co)):
                                        forward[y, zl, z2, s, k2, y2, c2, par, t, kk] = value
                                    for s, t, value in ((0, 0, co), (0, 1, -si), (1, 0, si), (1, 1, co)):
                                        inverse[y, zl, z2, t, k2, y2, c2, par, s, kk] = value
    return narrow_type(forward.reshape(32, 64, 128)), narrow_type(inverse.reshape(32, 64, 128))


def dot(a, b, dims):
    return lax.dot_general(a, b, ((dims[:1], dims[1:]), ((), ())), preferred_element_type=F32)


def gelu_parts(v):
    cumulative = 0.5 * (1.0 + lax.erf(v * (1.0 / math.sqrt(2.0))))
    bell = jnp.exp(-0.5 * v * v) * (1.0 / math.sqrt(2.0 * math.pi))
    return v * cumulative, cumulative + v * bell


def column(row, rows):
    return jnp.transpose(jnp.broadcast_to(row, (128, rows)))


def kernel(
    v_hbm, w_hbm, mix_hbm, bias_hbm, head_hbm, hb_hbm, ow_hbm, cot_hbm, ez_hbm, ei_hbm, r_hbm, t1_hbm, t2_hbm,
    pred_out, field_out, spec_out, mixg_out, headg_out,
    v_in, w_in, mix_in, bias_in, head_in, hb_in, ow_in, cot_in, ez_in, ei_in, r_rows, t1_in, t2_in, r_in,
    vf, vy, wst, wcat, mixed, hidden, gp, slope, gpre, fin, lhs, zrow, srow, arow,
    pred_s, field_s, spec_s, mixg_s, headg_s,
    asend, arecv, bsend, brecv, csend, crecv, dsend, drecv,
    g1send, g1recv, g2send, g2recv, g3recv,
    in_sem, out_sem, send_sem, recv_sem,
):
    w = lax.axis_index("wide")
    n = lax.axis_index("narrow")
    y, zl, c = w // 16, lax.rem(w // 2, 8), lax.rem(w, 2)
    x, zh = n // 2, lax.rem(n, 2)
    q = x * 8 + y * 2 + c
    z = zh * 8 + zl

    cross = []
    for dx, dy, dc in CROSS:
        x2, y2, c2 = lax.rem(x + dx, 4), lax.rem(y + dy, 4), lax.rem(c + dc, 2)
        cross.append((x2, y2, c2, (y2 * 16 + zl * 2 + c2, x2 * 2 + zh)))
    ring = []
    for d in RING:
        z2 = lax.rem(z + d, 16)
        ring.append((z2, (y * 16 + lax.rem(z2, 8) * 2 + c, x * 2 + z2 // 8)))

    barrier = pltpu.get_barrier_semaphore()
    for *_, where in ring:
        pl.semaphore_signal(barrier, inc=1, device_id=where, device_id_type=MESH)
    for *_, where in cross:
        pl.semaphore_signal(barrier, inc=1, device_id=where, device_id_type=MESH)

    variant = y * 8 + zl
    loads = [
        (v_hbm, v_in), (ez_hbm, ez_in), (r_hbm.at[n], r_rows), (t1_hbm.at[variant], t1_in), (w_hbm, w_in),
        (mix_hbm, mix_in), (bias_hbm, bias_in), (head_hbm, head_in), (hb_hbm, hb_in), (ow_hbm, ow_in),
        (cot_hbm, cot_in), (ei_hbm, ei_in), (t2_hbm.at[variant], t2_in),
    ]
    loads = [pltpu.make_async_copy(a, b, in_sem.at[i]) for i, (a, b) in enumerate(loads)]
    for load in loads:
        load.start()

    def send(source, target, where, stage):
        pltpu.make_async_remote_copy(
            src_ref=source, dst_ref=target, send_sem=send_sem.at[stage], recv_sem=recv_sem.at[stage],
            device_id=where, device_id_type=MESH,
        ).start()

    def arrived(buffer, count, stage):
        part = buffer.at[pl.ds(0, count)]
        pltpu.make_async_copy(part, part, recv_sem.at[stage]).wait()

    def sent(buffer, count, stage):
        part = buffer.at[pl.ds(0, count)]
        pltpu.make_async_copy(part, part, send_sem.at[stage]).wait()

    def local_analysis(values, flag, turn):
        spectra = dot(ez_in[flag], values, (1, 1)).astype(BF)
        planes = dot(spectra[:32], r_in[:256], (1, 0)) + dot(spectra[32:], r_in[256:], (1, 0))
        for x2 in range(4):
            for c2 in range(2):
                first = planes[8 * x2 : 8 * x2 + 8, 256 * c2 : 256 * c2 + 128]
                second = planes[8 * x2 : 8 * x2 + 8, 256 * c2 + 128 : 256 * c2 + 256]
                asend[turn, x2 * 2 + c2] = jnp.concatenate([first, second], axis=0).astype(BF)
        arecv[turn, q] = asend[turn, x * 2 + c]

    def analysis_send(turn):
        for x2, y2, c2, where in cross:
            send(asend.at[turn, x2 * 2 + c2], arecv.at[turn, q], where, 4 * turn)

    def analysis_middle(turn):
        arrived(arecv.at[turn], 31, 4 * turn)
        table = t1_in[...]
        table = jnp.concatenate([table] * 4, axis=1)
        partial = dot(table, arecv[turn].reshape(512, 128), (1, 0))
        for z2 in range(16):
            bsend[turn, z2] = partial[4 * z2 : 4 * z2 + 4]
        brecv[turn, z] = bsend[turn, z]
        for z2, where in ring:
            send(bsend.at[turn, z2], brecv.at[turn, z], where, 4 * turn + 1)

    def analysis_end(turn):
        arrived(brecv.at[turn], 15, 4 * turn + 1)
        total = brecv[turn, 0]
        for z2 in range(1, 16):
            total = total + brecv[turn, z2]
        return total

    def paired(spectrum, low_sign, high_sign):
        srow[0:2] = low_sign * spectrum[2:4]
        srow[2:4] = high_sign * spectrum[0:2]
        turned = srow[0:4]
        row = lax.broadcasted_iota(jnp.int32, (4, 128), 0)
        even = lax.rem(row, 2) == 0
        parts = [
            jnp.where(even, spectrum, 0.0), jnp.where(even, turned, 0.0),
            jnp.where(even, 0.0, spectrum), jnp.where(even, 0.0, turned),
        ]
        return jnp.concatenate(parts, axis=1).astype(BF)

    def synthesis_start(modes, turn):
        csend[turn] = modes
        crecv[turn, z] = modes
        for z2, where in ring:
            send(csend.at[turn], crecv.at[turn, z], where, 4 * turn + 2)

    def synthesis_middle(turn):
        arrived(crecv.at[turn], 15, 4 * turn + 2)
        for z2 in range(16):
            zrow[4 * z2 : 4 * z2 + 4] = crecv[turn, z2]
        planes = dot(t2_in[...], zrow[...].astype(BF), (0, 0)).astype(BF)
        for piece in range(8):
            dsend[turn, piece] = planes[16 * piece : 16 * piece + 16]
        drecv[turn, q] = dsend[turn, y * 2 + c]
        for x2, y2, c2, where in cross:
            send(dsend.at[turn, y2 * 2 + c2], drecv.at[turn, q], where, 4 * turn + 3)

    def synthesis_end(flag, turn):
        arrived(drecv.at[turn], 31, 4 * turn + 3)
        for x2 in range(4):
            for c2 in range(2):
                block = drecv[turn, x2 * 8 + c2].astype(F32)
                for y2 in range(1, 4):
                    block = block + drecv[turn, x2 * 8 + y2 * 2 + c2].astype(F32)
                lhs[8 * x2 : 8 * x2 + 8, 256 * c2 : 256 * c2 + 128] = block[:8]
                lhs[8 * x2 : 8 * x2 + 8, 256 * c2 + 128 : 256 * c2 + 256] = block[8:]
        lines = dot(lhs[...].astype(BF), r_in[...], (1, 1)).astype(BF)
        stacked = jnp.concatenate([lines[:, :256], lines[:, 256:]], axis=0)
        return dot(stacked, ei_in[flag], (0, 0))

    for i in (0, 1, 2):
        loads[i].wait()
    keep = lax.rem(lax.broadcasted_iota(jnp.int32, (32, 512), 1), 32) == lax.broadcasted_iota(jnp.int32, (32, 512), 0)
    for row in range(16):
        spread = jnp.broadcast_to(r_rows[row : row + 1], (32, 512))
        r_in[32 * row : 32 * row + 32] = jnp.where(keep, spread, 0.0).astype(BF)
    vf[...] = v_in[...].astype(F32)
    for row in range(8):
        vy[32 * row : 32 * row + 32] = vf[pl.ds(row, 32, stride=8), :].astype(BF)
    local_analysis(vy[...], 0, 0)

    for load in loads[3:]:
        load.wait()
    for k2 in range(2):
        for r in range(2):
            for j4 in range(4):
                block = w_in[j4, k2, r].astype(BF)
                zero = jnp.zeros((32, 32), BF)
                wide = jnp.concatenate([zero] * j4 + [block] + [zero] * (3 - j4), axis=1)
                base = 128 * (2 * k2 + r)
                wst[base + 32 * j4 : base + 32 * j4 + 32] = wide
                wcat[32 * j4 : 32 * j4 + 32, base : base + 128] = wide
    bias_col = column(bias_in[...], 32)
    for row in range(8):
        mixed[32 * row : 32 * row + 32] = dot(mix_in[...], vy[32 * row : 32 * row + 32], (0, 0)) + bias_col
    head_col = column(hb_in[...], 128)
    out_col = column(ow_in[...].astype(F32), 128)

    pl.semaphore_wait(barrier, len(CROSS) + len(RING))
    analysis_send(0)
    analysis_middle(0)
    spectrum = analysis_end(0)
    modes = dot(paired(spectrum, -1.0, 1.0), wst[...], (1, 0))
    synthesis_start(modes, 0)
    synthesis_middle(0)
    pre = synthesis_end(1, 0) + mixed[...]

    value, rate = gelu_parts(pre)
    hidden[...] = value.astype(BF)
    gp[...] = rate
    for row in range(8):
        head_pre = dot(head_in[...], hidden[32 * row : 32 * row + 32], (0, 0)) + head_col
        value, rate = gelu_parts(head_pre)
        pred_s[row : row + 1] = dot(ow_in[...], value.astype(BF), (1, 0))
        slope[128 * row : 128 * row + 128] = (cot_in[row : row + 1] * out_col * rate).astype(BF)
        back = dot(head_in[...], slope[128 * row : 128 * row + 128], (1, 0))
        gpre[32 * row : 32 * row + 32] = (back * gp[32 * row : 32 * row + 32]).astype(BF)
    stores = [pltpu.make_async_copy(pred_s, pred_out, out_sem.at[0])]
    stores[0].start()
    local_analysis(gpre[...], 1, 1)
    analysis_send(1)

    head_grad = jnp.zeros((32, 128), F32)
    mix_grad = jnp.zeros((32, 32), F32)
    for row in range(8):
        head_grad = head_grad + dot(hidden[32 * row : 32 * row + 32], slope[128 * row : 128 * row + 128], (1, 1))
        mix_grad = mix_grad + dot(vy[32 * row : 32 * row + 32], gpre[32 * row : 32 * row + 32], (1, 1))
    folded = jnp.concatenate([mix_grad[8 * i : 8 * i + 8] for i in range(4)], axis=1)
    for i in range(16):
        g1send[i] = head_grad[2 * i : 2 * i + 2]
    for i in range(4):
        g1send[16 + i] = folded[2 * i : 2 * i + 2]
    for i in range(20, 32):
        g1send[i] = jnp.zeros((2, 128), F32)
    g1recv[q] = g1send[q]
    for x2, y2, c2, where in cross:
        send(g1send.at[x2 * 8 + y2 * 2 + c2], g1recv.at[q], where, 8)
    for row in range(8):
        mixed[32 * row : 32 * row + 32] = dot(mix_in[...], gpre[32 * row : 32 * row + 32], (1, 0))

    analysis_middle(1)

    arrived(g1recv, 31, 8)
    total = g1recv[0]
    for i in range(1, 32):
        total = total + g1recv[i]
    g2send[...] = total
    g2recv[z] = total
    for z2, where in ring:
        send(g2send, g2recv.at[z], where, 9)

    adjoint = analysis_end(1)
    modes = dot(paired(adjoint, 1.0, -1.0), wcat[...], (1, 1))
    synthesis_start(modes, 1)

    arrived(g2recv, 15, 9)
    total = g2recv[0]
    for i in range(1, 16):
        total = total + g2recv[i]
    g3recv[q] = total
    for x2, y2, c2, where in cross:
        send(g3recv.at[q], g3recv.at[q], where, 10)

    for j4 in range(4):
        arow[4 * j4 : 4 * j4 + 4] = adjoint[:, 32 * j4 : 32 * j4 + 32]
    rows = lax.broadcasted_iota(jnp.int32, (16, 128), 0)
    lanes = lax.broadcasted_iota(jnp.int32, (16, 128), 1)
    diagonal = rows // 4 == lanes // 32
    targets = arow[...].astype(BF)
    part = lax.rem(rows, 4)
    for k2 in range(2):
        real = jnp.broadcast_to(spectrum[k2 : k2 + 1], (16, 128))
        imag = jnp.broadcast_to(spectrum[2 + k2 : 3 + k2], (16, 128))
        for r in range(2):
            on_real = real if r == 0 else -imag
            on_imag = imag if r == 0 else real
            left = jnp.where(part == k2, on_real, jnp.where(part == 2 + k2, on_imag, 0.0))
            left = jnp.where(diagonal, left, 0.0).astype(BF)
            product = dot(left, targets, (0, 0))
            for j4 in range(4):
                spec_s[j4, k2, r] = product[32 * j4 : 32 * j4 + 32]
    stores.append(pltpu.make_async_copy(spec_s, spec_out, out_sem.at[1]))
    stores[1].start()

    synthesis_middle(1)

    arrived(g3recv, 31, 10)
    for i in range(16):
        headg_s[2 * i : 2 * i + 2] = g3recv[i]
    for i in range(4):
        rows2 = g3recv[16 + i]
        for j in range(4):
            mixg_s[8 * j + 2 * i : 8 * j + 2 * i + 2] = rows2[:, 32 * j : 32 * j + 32]
    stores.append(pltpu.make_async_copy(mixg_s, mixg_out, out_sem.at[2]))
    stores.append(pltpu.make_async_copy(headg_s, headg_out, out_sem.at[3]))
    stores[2].start()
    stores[3].start()

    field = synthesis_end(0, 1) + mixed[...]
    for row in range(8):
        fin[pl.ds(row, 32, stride=8), :] = field[32 * row : 32 * row + 32]
    field_s[...] = fin[...].astype(BF)
    stores.append(pltpu.make_async_copy(field_s, field_out, out_sem.at[4]))
    stores[4].start()

    for turn in range(2):
        sent(arecv.at[turn], 31, 4 * turn)
        sent(brecv.at[turn], 15, 4 * turn + 1)
        sent(crecv.at[turn], 15, 4 * turn + 2)
        sent(drecv.at[turn], 31, 4 * turn + 3)
    sent(g1recv, 31, 8)
    sent(g2recv, 15, 9)
    sent(g3recv, 31, 10)
    for store in stores:
        store.wait()


def body(lifted_field, spectral_weight, mix_weight, mix_bias, head_weight, head_bias, out_weight, cotangent):
    forward_z, inverse_z = z_tables()
    forward_x, inverse_x = x_tables()
    inputs = (
        lifted_field.reshape(256, 128), spectral_weight, mix_weight, mix_bias.reshape(1, 32), head_weight,
        head_bias.reshape(1, 128), out_weight.reshape(1, 128), cotangent.reshape(8, 128),
        jnp.asarray(forward_z), jnp.asarray(inverse_z), jnp.asarray(y_tables()), jnp.asarray(forward_x), jnp.asarray(inverse_x),
    )
    whole = lambda a: pltpu.VMEM(a.shape, a.dtype)
    tail = lambda a: pltpu.VMEM(a.shape[1:], a.dtype)
    outputs = [
        jax.ShapeDtypeStruct((8, 128), F32), jax.ShapeDtypeStruct((256, 128), BF),
        jax.ShapeDtypeStruct((4, 2, 2, 32, 32), F32), jax.ShapeDtypeStruct((32, 32), F32), jax.ShapeDtypeStruct((32, 128), F32),
    ]
    scratch = [whole(a) for a in inputs[:10]] + [tail(a) for a in inputs[10:]] + [pltpu.VMEM((512, 512), BF)]
    scratch += [
        pltpu.VMEM((256, 128), F32), pltpu.VMEM((256, 128), BF), pltpu.VMEM((512, 128), BF), pltpu.VMEM((128, 512), BF),
        pltpu.VMEM((256, 128), F32), pltpu.VMEM((256, 128), BF), pltpu.VMEM((256, 128), F32), pltpu.VMEM((1024, 128), BF),
        pltpu.VMEM((256, 128), BF), pltpu.VMEM((256, 128), F32), pltpu.VMEM((32, 512), F32), pltpu.VMEM((64, 128), F32),
        pltpu.VMEM((8, 128), F32), pltpu.VMEM((16, 32), F32),
    ]
    scratch += [whole(a) for a in outputs]
    scratch += [
        pltpu.VMEM((2, 8, 16, 128), BF), pltpu.VMEM((2, 32, 16, 128), BF),
        pltpu.VMEM((2, 16, 4, 128), F32), pltpu.VMEM((2, 16, 4, 128), F32),
        pltpu.VMEM((2, 4, 128), F32), pltpu.VMEM((2, 16, 4, 128), F32),
        pltpu.VMEM((2, 8, 16, 128), BF), pltpu.VMEM((2, 32, 16, 128), BF),
        pltpu.VMEM((32, 2, 128), F32), pltpu.VMEM((32, 2, 128), F32),
        pltpu.VMEM((2, 128), F32), pltpu.VMEM((16, 2, 128), F32), pltpu.VMEM((32, 2, 128), F32),
        pltpu.SemaphoreType.DMA((13,)), pltpu.SemaphoreType.DMA((5,)), pltpu.SemaphoreType.DMA((11,)), pltpu.SemaphoreType.DMA((11,)),
    ]
    prediction, field, spectral, mix_grad, head_grad = pl.pallas_call(
        kernel,
        out_shape=outputs,
        in_specs=[pl.BlockSpec(memory_space=pltpu.HBM)] * len(inputs),
        out_specs=[pl.BlockSpec(memory_space=pltpu.HBM)] * len(outputs),
        scratch_shapes=scratch,
        name="step",
        compiler_params=pltpu.CompilerParams(collective_id=0, has_side_effects=True),
    )(*inputs)
    return prediction.reshape(1, 8, 128), field.reshape(1, 32, 8, 128), spectral, mix_grad, head_grad


def solution(mesh):
    return jax.shard_map(
        body,
        mesh=mesh,
        in_specs=(
            P("wide", None, "narrow", None),
            P("wide", "narrow", None, None, None),
            P(),
            P(),
            P(),
            P(),
            P(),
            P("wide", "narrow", None),
        ),
        out_specs=(
            P("wide", "narrow", None),
            P("wide", None, "narrow", None),
            P("wide", "narrow", None, None, None),
            P(),
            P(),
        ),
        check_vma=False,
    )
```

```python
import functools
import math

import jax
import jax.numpy as jnp
import ml_dtypes
import numpy as np
from jax import lax
from jax.experimental import pallas as pl
from jax.experimental.pallas import tpu as pltpu
from jax.sharding import PartitionSpec as P

MESH = pl.DeviceIdType.MESH
BF = jnp.bfloat16
F32 = jnp.float32
NX, NY, NZ, C, HID = 64, 64, 128, 32, 128
CROSS = [(dx, dy, dc) for dx in range(4) for dy in range(4) for dc in range(2) if dx or dy or dc]
CROSS.sort(key=lambda t: (-(min(t[0], 4 - t[0]) + min(t[1], 4 - t[1])), t))
RING = sorted(range(1, 16), key=lambda d: (-min(d, 16 - d), d))


def angle(position, frequency, length):
    return 2.0 * math.pi * ((position * frequency) % length) / length


def narrow_type(table):
    return np.asarray(table, np.float32).astype(ml_dtypes.bfloat16)


@functools.lru_cache(None)
def z_tables():
    forward = np.zeros((2, 2, 4, 2, 4, NZ))
    inverse = np.zeros((2, 2, 4, 2, 4, NZ))
    z = np.arange(NZ)
    for flag in range(2):
        for k in range(16):
            scale = (2.0 if flag and k else 1.0) / math.sqrt(NZ)
            real, imag = scale * np.cos(angle(z, k, NZ)), -scale * np.sin(angle(z, k, NZ))
            x, kk = k // 4, k % 4
            forward[flag, 0, x, 0, kk], forward[flag, 0, x, 1, kk] = real, imag
            forward[flag, 1, x, 0, kk], forward[flag, 1, x, 1, kk] = imag, -real
            inverse[flag, 0, x, 0, kk], inverse[flag, 0, x, 1, kk] = real, imag
            inverse[flag, 1, x, 0, kk], inverse[flag, 1, x, 1, kk] = imag, -real
    return narrow_type(forward.reshape(2, 64, NZ)), narrow_type(inverse.reshape(2, 64, NZ))


def frequency(i):
    return i if i < 8 else i - 16


@functools.lru_cache(None)
def y_tables():
    out = np.zeros((8, 2, 8, 16, C), np.float32)
    for n in range(8):
        for y in range(8):
            for place in range(16):
                core, par, low = place // 8, (place // 4) % 2, place % 4
                theta = angle(8 * n + y, frequency((2 * par + core) * 4 + low), NY)
                out[n, 0, y, place] = math.cos(theta) / 8.0
                out[n, 1, y, place] = math.sin(theta) / 8.0
    return out.reshape(8, 16, 512)


@functools.lru_cache(None)
def x_tables():
    forward = np.zeros((4, 8, 4, 4, 2, 2, 4, 2, 2, 2, 4), np.float32)
    inverse = np.zeros((4, 8, 4, 4, 2, 2, 4, 2, 2, 2, 4), np.float32)
    for y in range(4):
        for zl in range(8):
            for i4 in range(4):
                for y2 in range(4):
                    for c2 in range(2):
                        theta = angle(16 * y2 + 2 * zl + c2, frequency(4 * y + i4), NX)
                        co, si = math.cos(theta) / 8.0, math.sin(theta) / 8.0
                        for par in range(2):
                            for zh in range(2):
                                for k2 in range(2):
                                    kk, kind, block = 2 * zh + k2, (2 * i4 + par) % 4, 2 * zh + i4 // 2
                                    for s, t, value in ((0, 0, co), (0, 1, si), (1, 0, -si), (1, 1, co)):
                                        forward[y, zl, kind, block, s, k2, y2, c2, par, t, kk] = value
                                    for s, t, value in ((0, 0, co), (0, 1, -si), (1, 0, si), (1, 1, co)):
                                        inverse[y, zl, kind, block, t, k2, y2, c2, par, s, kk] = value
    return narrow_type(forward.reshape(32, 64, 128)), narrow_type(inverse.reshape(32, 64, 128))


def dot(a, b, dims):
    return lax.dot_general(a, b, ((dims[:1], dims[1:]), ((), ())), preferred_element_type=F32)


def gelu_parts(v):
    cumulative = 0.5 * (1.0 + lax.erf(v * (1.0 / math.sqrt(2.0))))
    bell = jnp.exp(-0.5 * v * v) * (1.0 / math.sqrt(2.0 * math.pi))
    return v * cumulative, cumulative + v * bell


def column(row, rows):
    return jnp.transpose(jnp.broadcast_to(row, (128, rows)))


def kernel(
    v_hbm, w_hbm, mix_hbm, bias_hbm, head_hbm, hb_hbm, ow_hbm, cot_hbm, ez_hbm, ei_hbm, r_hbm, t1_hbm, t2_hbm,
    pred_out, field_out, spec_out, mixg_out, headg_out,
    v_in, w_in, mix_in, bias_in, head_in, hb_in, ow_in, cot_in, ez_in, ei_in, r_rows, t1_in, t2_in, r_in,
    vf, vy, wflat, wall, wst, wcat, mixed, hidden, gp, slope, gpre, fin, lhs, srow, arow, own,
    asend, arecv, bsend, brecv, crecv, dsend, drecv,
    g1send, g1recv, g2send, g2recv, g3recv,
    in_sem, send_sem, recv_sem,
):
    w = lax.axis_index("wide")
    n = lax.axis_index("narrow")
    y, zl, c = w // 16, lax.rem(w // 2, 8), lax.rem(w, 2)
    x, zh = n // 2, lax.rem(n, 2)
    q = x * 8 + y * 2 + c
    z = zh * 8 + zl
    kind, block = lax.rem(zl, 4), 2 * zh + zl // 4

    cross = []
    for dx, dy, dc in CROSS:
        x2, y2, c2 = lax.rem(x + dx, 4), lax.rem(y + dy, 4), lax.rem(c + dc, 2)
        cross.append((x2, y2, c2, (y2 * 16 + zl * 2 + c2, x2 * 2 + zh)))
    ring = []
    for d in RING:
        z2 = lax.rem(z + d, 16)
        ring.append((z2, (y * 16 + lax.rem(z2, 8) * 2 + c, x * 2 + z2 // 8)))
    near = [ring[RING.index(d)][1] for d in (14, 1, 15)]
    alike = [ring[RING.index(d)][1] for d in (8, 4, 12)]

    barrier = pltpu.get_barrier_semaphore()
    for *_, where in ring:
        pl.semaphore_signal(barrier, inc=1, device_id=where, device_id_type=MESH)
    for *_, where in cross:
        pl.semaphore_signal(barrier, inc=1, device_id=where, device_id_type=MESH)

    variant = y * 8 + zl
    loads = [
        (v_hbm, v_in), (ez_hbm, ez_in), (r_hbm.at[n], r_rows), (t1_hbm.at[variant], t1_in), (w_hbm, w_in),
        (mix_hbm, mix_in), (bias_hbm, bias_in), (head_hbm, head_in), (hb_hbm, hb_in), (ow_hbm, ow_in),
        (cot_hbm, cot_in), (ei_hbm, ei_in), (t2_hbm.at[variant], t2_in),
    ]
    loads = [pltpu.make_async_copy(a, b, in_sem.at[i]) for i, (a, b) in enumerate(loads)]
    for load in loads:
        load.start()

    def send(source, target, where, stage):
        pltpu.make_async_remote_copy(
            src_ref=source, dst_ref=target, send_sem=send_sem.at[stage], recv_sem=recv_sem.at[stage],
            device_id=where, device_id_type=MESH,
        ).start()

    def arrived(buffer, count, stage):
        part = buffer.at[pl.ds(0, count)]
        pltpu.make_async_copy(part, part, recv_sem.at[stage]).wait()

    def sent(buffer, count, stage):
        part = buffer.at[pl.ds(0, count)]
        pltpu.make_async_copy(part, part, send_sem.at[stage]).wait()

    def local_analysis(values, flag, turn):
        spectra = dot(ez_in[flag], values, (1, 1)).astype(BF)
        planes = dot(spectra[:32], r_in[:256], (1, 0)) + dot(spectra[32:], r_in[256:], (1, 0))
        for x2 in range(4):
            for c2 in range(2):
                first = planes[8 * x2 : 8 * x2 + 8, 256 * c2 : 256 * c2 + 128]
                second = planes[8 * x2 : 8 * x2 + 8, 256 * c2 + 128 : 256 * c2 + 256]
                asend[turn, x2 * 2 + c2] = jnp.concatenate([first, second], axis=0).astype(BF)
        arecv[turn, q] = asend[turn, x * 2 + c]

    def analysis_send(turn):
        for x2, y2, c2, where in cross:
            send(asend.at[turn, x2 * 2 + c2], arecv.at[turn, q], where, 4 * turn)

    def analysis_middle(turn):
        arrived(arecv.at[turn], 31, 4 * turn)
        table = t1_in[...]
        table = jnp.concatenate([table] * 4, axis=1)
        partial = dot(table, arecv[turn].reshape(512, 128), (1, 0)).astype(BF)
        for piece in range(4):
            bsend[turn, piece] = partial[16 * piece : 16 * piece + 16]
        brecv[turn, z] = bsend[turn, kind]
        for z2, where in ring:
            send(bsend.at[turn, lax.rem(z2, 4)], brecv.at[turn, z], where, 4 * turn + 1)

    def analysis_end(turn):
        arrived(brecv.at[turn], 15, 4 * turn + 1)
        total = brecv[turn, 0].astype(F32)
        for z2 in range(1, 16):
            total = total + brecv[turn, z2].astype(F32)
        for i in range(4):
            own[turn, i] = total[4 * i : 4 * i + 4]
        return total

    def paired(spectrum, low_sign, high_sign):
        for i in range(4):
            srow[4 * i : 4 * i + 2] = low_sign * spectrum[4 * i + 2 : 4 * i + 4]
            srow[4 * i + 2 : 4 * i + 4] = high_sign * spectrum[4 * i : 4 * i + 2]
        turned = srow[...]
        row = lax.broadcasted_iota(jnp.int32, (16, 128), 0)
        parts = []
        for i in range(4):
            for k2 in range(2):
                mine = (row // 4 == i) & (lax.rem(row, 2) == k2)
                parts += [jnp.where(mine, spectrum, 0.0), jnp.where(mine, turned, 0.0)]
        return jnp.concatenate(parts, axis=1).astype(BF)

    def synthesis_start(modes, turn):
        crecv[turn, kind] = modes.astype(BF)
        for where in near:
            send(crecv.at[turn, kind], crecv.at[turn, kind], where, 4 * turn + 2)

    def synthesis_middle(turn):
        arrived(crecv.at[turn], 3, 4 * turn + 2)
        planes = dot(t2_in[...], crecv[turn].reshape(64, 128), (0, 0)).astype(BF)
        for piece in range(8):
            dsend[turn, piece] = planes[16 * piece : 16 * piece + 16]
        drecv[turn, q] = dsend[turn, y * 2 + c]
        for x2, y2, c2, where in cross:
            send(dsend.at[turn, y2 * 2 + c2], drecv.at[turn, q], where, 4 * turn + 3)

    def synthesis_end(flag, turn):
        arrived(drecv.at[turn], 31, 4 * turn + 3)
        for x2 in range(4):
            for c2 in range(2):
                block = drecv[turn, x2 * 8 + c2].astype(F32)
                for y2 in range(1, 4):
                    block = block + drecv[turn, x2 * 8 + y2 * 2 + c2].astype(F32)
                lhs[8 * x2 : 8 * x2 + 8, 256 * c2 : 256 * c2 + 128] = block[:8]
                lhs[8 * x2 : 8 * x2 + 8, 256 * c2 + 128 : 256 * c2 + 256] = block[8:]
        lines = dot(lhs[...].astype(BF), r_in[...], (1, 1)).astype(BF)
        stacked = jnp.concatenate([lines[:, :256], lines[:, 256:]], axis=0)
        return dot(stacked, ei_in[flag], (0, 0))

    for i in (0, 1, 2):
        loads[i].wait()
    keep = lax.rem(lax.broadcasted_iota(jnp.int32, (32, 512), 1), 32) == lax.broadcasted_iota(jnp.int32, (32, 512), 0)
    for row in range(16):
        spread = jnp.broadcast_to(r_rows[row : row + 1], (32, 512))
        r_in[32 * row : 32 * row + 32] = jnp.where(keep, spread, 0.0).astype(BF)
    vf[...] = v_in[...].astype(F32)
    for row in range(8):
        vy[32 * row : 32 * row + 32] = vf[pl.ds(row, 32, stride=8), :].astype(BF)
    local_analysis(vy[...], 0, 0)

    for load in loads[3:]:
        load.wait()
    for j4 in range(4):
        for k2 in range(2):
            for r in range(2):
                base = 128 * (2 * k2 + r) + 32 * j4
                wflat[:, base : base + 32] = w_in[j4, k2, r]
    wall[block] = wflat[...].astype(BF)
    bias_col = column(bias_in[...], 32)
    for row in range(8):
        mixed[32 * row : 32 * row + 32] = dot(mix_in[...], vy[32 * row : 32 * row + 32], (0, 0)) + bias_col
    head_col = column(hb_in[...], 128)
    out_col = column(ow_in[...].astype(F32), 128)

    pl.semaphore_wait(barrier, len(CROSS) + len(RING))
    analysis_send(0)
    for where in alike:
        send(wall.at[block], wall.at[block], where, 11)
    analysis_middle(0)
    arrived(wall, 3, 11)
    inside = lax.broadcasted_iota(jnp.int32, (128, 128), 0) // 32 == lax.broadcasted_iota(jnp.int32, (128, 128), 1) // 32
    for i in range(4):
        for part in range(4):
            compact = wall[i, :, 128 * part : 128 * part + 128].astype(F32)
            full = jnp.where(inside, jnp.concatenate([compact] * 4, axis=0), 0.0).astype(BF)
            base = 128 * (4 * i + part)
            wst[base : base + 128] = full
            wcat[:, base : base + 128] = full
    modes = dot(paired(analysis_end(0), -1.0, 1.0), wst[...], (1, 0))
    synthesis_start(modes, 0)
    synthesis_middle(0)
    pre = synthesis_end(1, 0) + mixed[...]

    value, rate = gelu_parts(pre)
    hidden[...] = value.astype(BF)
    gp[...] = rate
    for row in range(8):
        head_pre = dot(head_in[...], hidden[32 * row : 32 * row + 32], (0, 0)) + head_col
        value, rate = gelu_parts(head_pre)
        pred_out[row : row + 1] = dot(ow_in[...], value.astype(BF), (1, 0))
        slope[128 * row : 128 * row + 128] = (cot_in[row : row + 1] * out_col * rate).astype(BF)
        back = dot(head_in[...], slope[128 * row : 128 * row + 128], (1, 0))
        gpre[32 * row : 32 * row + 32] = (back * gp[32 * row : 32 * row + 32]).astype(BF)
    local_analysis(gpre[...], 1, 1)
    analysis_send(1)

    head_grad = jnp.zeros((32, 128), F32)
    mix_grad = jnp.zeros((32, 32), F32)
    for row in range(8):
        head_grad = head_grad + dot(hidden[32 * row : 32 * row + 32], slope[128 * row : 128 * row + 128], (1, 1))
        mix_grad = mix_grad + dot(vy[32 * row : 32 * row + 32], gpre[32 * row : 32 * row + 32], (1, 1))
    folded = jnp.concatenate([mix_grad[8 * i : 8 * i + 8] for i in range(4)], axis=1)
    for i in range(16):
        g1send[i] = head_grad[2 * i : 2 * i + 2]
    for i in range(4):
        g1send[16 + i] = folded[2 * i : 2 * i + 2]
    for i in range(20, 32):
        g1send[i] = jnp.zeros((2, 128), F32)
    g1recv[q] = g1send[q]
    for x2, y2, c2, where in cross:
        send(g1send.at[x2 * 8 + y2 * 2 + c2], g1recv.at[q], where, 8)
    for row in range(8):
        mixed[32 * row : 32 * row + 32] = dot(mix_in[...], gpre[32 * row : 32 * row + 32], (1, 0))

    analysis_middle(1)

    arrived(g1recv, 31, 8)
    total = g1recv[0]
    for i in range(1, 32):
        total = total + g1recv[i]
    g2send[...] = total
    g2recv[z] = total
    for z2, where in ring:
        send(g2send, g2recv.at[z], where, 9)

    modes = dot(paired(analysis_end(1), 1.0, -1.0), wcat[...], (1, 1))
    synthesis_start(modes, 1)
    spectrum = own[0, block]
    adjoint = own[1, block]

    arrived(g2recv, 15, 9)
    total = g2recv[0]
    for i in range(1, 16):
        total = total + g2recv[i]
    g3recv[q] = total
    for x2, y2, c2, where in cross:
        send(g3recv.at[q], g3recv.at[q], where, 10)

    for j4 in range(4):
        arow[4 * j4 : 4 * j4 + 4] = adjoint[:, 32 * j4 : 32 * j4 + 32]
    rows = lax.broadcasted_iota(jnp.int32, (16, 128), 0)
    lanes = lax.broadcasted_iota(jnp.int32, (16, 128), 1)
    diagonal = rows // 4 == lanes // 32
    targets = arow[...].astype(BF)
    part = lax.rem(rows, 4)
    for k2 in range(2):
        real = jnp.broadcast_to(spectrum[k2 : k2 + 1], (16, 128))
        imag = jnp.broadcast_to(spectrum[2 + k2 : 3 + k2], (16, 128))
        for r in range(2):
            on_real = real if r == 0 else -imag
            on_imag = imag if r == 0 else real
            left = jnp.where(part == k2, on_real, jnp.where(part == 2 + k2, on_imag, 0.0))
            left = jnp.where(diagonal, left, 0.0).astype(BF)
            product = dot(left, targets, (0, 0))
            for j4 in range(4):
                spec_out[j4, k2, r] = product[32 * j4 : 32 * j4 + 32]

    synthesis_middle(1)

    arrived(g3recv, 31, 10)
    for i in range(16):
        headg_out[2 * i : 2 * i + 2] = g3recv[i]
    for i in range(4):
        rows2 = g3recv[16 + i]
        for j in range(4):
            mixg_out[8 * j + 2 * i : 8 * j + 2 * i + 2] = rows2[:, 32 * j : 32 * j + 32]

    field = synthesis_end(0, 1) + mixed[...]
    for row in range(8):
        fin[pl.ds(row, 32, stride=8), :] = field[32 * row : 32 * row + 32]
    field_out[...] = fin[...].astype(BF)

    for turn in range(2):
        sent(arecv.at[turn], 31, 4 * turn)
        sent(brecv.at[turn], 15, 4 * turn + 1)
        sent(crecv.at[turn], 3, 4 * turn + 2)
        sent(drecv.at[turn], 31, 4 * turn + 3)
    sent(g1recv, 31, 8)
    sent(g2recv, 15, 9)
    sent(g3recv, 31, 10)
    sent(wall, 3, 11)


def publish(*refs):
    sem = refs[-1]
    copies = [pltpu.make_async_copy(refs[i], refs[5 + i], sem.at[i]) for i in (2, 1, 0, 3, 4)]
    for copy in copies:
        copy.start()
    for copy in copies:
        copy.wait()


def body(lifted_field, spectral_weight, mix_weight, mix_bias, head_weight, head_bias, out_weight, cotangent):
    forward_z, inverse_z = z_tables()
    forward_x, inverse_x = x_tables()
    inputs = (
        lifted_field.reshape(256, 128), spectral_weight, mix_weight, mix_bias.reshape(1, 32), head_weight,
        head_bias.reshape(1, 128), out_weight.reshape(1, 128), cotangent.reshape(8, 128),
        jnp.asarray(forward_z), jnp.asarray(inverse_z), jnp.asarray(y_tables()), jnp.asarray(forward_x), jnp.asarray(inverse_x),
    )
    inputs = tuple(pltpu.with_memory_space_constraint(a, pltpu.HBM) for a in inputs)
    whole = lambda a: pltpu.VMEM(a.shape, a.dtype)
    tail = lambda a: pltpu.VMEM(a.shape[1:], a.dtype)
    outputs = [
        jax.ShapeDtypeStruct((8, 128), F32), jax.ShapeDtypeStruct((256, 128), BF),
        jax.ShapeDtypeStruct((4, 2, 2, 32, 32), F32), jax.ShapeDtypeStruct((32, 32), F32), jax.ShapeDtypeStruct((32, 128), F32),
    ]
    scratch = [whole(a) for a in inputs[:10]] + [tail(a) for a in inputs[10:]] + [pltpu.VMEM((512, 512), BF)]
    scratch += [
        pltpu.VMEM((256, 128), F32), pltpu.VMEM((256, 128), BF), pltpu.VMEM((32, 512), F32), pltpu.VMEM((4, 32, 512), BF),
        pltpu.VMEM((2048, 128), BF), pltpu.VMEM((128, 2048), BF),
        pltpu.VMEM((256, 128), F32), pltpu.VMEM((256, 128), BF), pltpu.VMEM((256, 128), F32), pltpu.VMEM((1024, 128), BF),
        pltpu.VMEM((256, 128), BF), pltpu.VMEM((256, 128), F32), pltpu.VMEM((32, 512), F32),
        pltpu.VMEM((16, 128), F32), pltpu.VMEM((16, 32), F32), pltpu.VMEM((2, 4, 4, 128), F32),
    ]
    scratch += [
        pltpu.VMEM((2, 8, 16, 128), BF), pltpu.VMEM((2, 32, 16, 128), BF),
        pltpu.VMEM((2, 4, 16, 128), BF), pltpu.VMEM((2, 16, 16, 128), BF), pltpu.VMEM((2, 4, 16, 128), BF),
        pltpu.VMEM((2, 8, 16, 128), BF), pltpu.VMEM((2, 32, 16, 128), BF),
        pltpu.VMEM((32, 2, 128), F32), pltpu.VMEM((32, 2, 128), F32),
        pltpu.VMEM((2, 128), F32), pltpu.VMEM((16, 2, 128), F32), pltpu.VMEM((32, 2, 128), F32),
        pltpu.SemaphoreType.DMA((13,)), pltpu.SemaphoreType.DMA((12,)), pltpu.SemaphoreType.DMA((12,)),
    ]
    results = pl.pallas_call(
        kernel,
        out_shape=outputs,
        in_specs=[pl.BlockSpec(memory_space=pltpu.HBM)] * len(inputs),
        out_specs=[pl.BlockSpec(memory_space=pltpu.VMEM)] * len(outputs),
        scratch_shapes=scratch,
        name="step",
        compiler_params=pltpu.CompilerParams(collective_id=0, has_side_effects=True, vmem_limit_bytes=32 << 20),
    )(*inputs)
    prediction, field, spectral, mix_grad, head_grad = pl.pallas_call(
        publish,
        out_shape=outputs,
        in_specs=[pl.BlockSpec(memory_space=pltpu.VMEM)] * len(outputs),
        out_specs=[pl.BlockSpec(memory_space=pltpu.HBM)] * len(outputs),
        scratch_shapes=[pltpu.SemaphoreType.DMA((5,))],
        name="publish",
        compiler_params=pltpu.CompilerParams(vmem_limit_bytes=4 << 20),
    )(*results)
    return prediction.reshape(1, 8, 128), field.reshape(1, 32, 8, 128), spectral, mix_grad, head_grad


def solution(mesh):
    return jax.shard_map(
        body,
        mesh=mesh,
        in_specs=(
            P("wide", None, "narrow", None),
            P("wide", "narrow", None, None, None),
            P(),
            P(),
            P(),
            P(),
            P(),
            P("wide", "narrow", None),
        ),
        out_specs=(
            P("wide", "narrow", None),
            P("wide", None, "narrow", None),
            P("wide", "narrow", None, None, None),
            P(),
            P(),
        ),
        check_vma=False,
    )
```

```python
import functools
import math

import jax
import jax.numpy as jnp
import ml_dtypes
import numpy as np
from jax import lax
from jax.experimental import pallas as pl
from jax.experimental.pallas import tpu as pltpu
from jax.sharding import PartitionSpec as P

MESH = pl.DeviceIdType.MESH
BF = jnp.bfloat16
F32 = jnp.float32
NX, NY, NZ, C, HID = 64, 64, 128, 32, 128
CROSS = [(dx, dy, dc) for dx in range(4) for dy in range(4) for dc in range(2) if dx or dy or dc]
CROSS.sort(key=lambda t: (-(min(t[0], 4 - t[0]) + min(t[1], 4 - t[1])), t))
RING = sorted(range(1, 16), key=lambda d: (-min(d, 16 - d), d))


def angle(position, frequency, length):
    return 2.0 * math.pi * ((position * frequency) % length) / length


def narrow_type(table):
    return np.asarray(table, np.float32).astype(ml_dtypes.bfloat16)


@functools.lru_cache(None)
def z_tables():
    forward = np.zeros((2, 2, 4, 2, 4, NZ))
    inverse = np.zeros((2, 2, 4, 2, 4, NZ))
    z = np.arange(NZ)
    for flag in range(2):
        for k in range(16):
            scale = (2.0 if flag and k else 1.0) / math.sqrt(NZ)
            real, imag = scale * np.cos(angle(z, k, NZ)), -scale * np.sin(angle(z, k, NZ))
            x, kk = k // 4, k % 4
            forward[flag, 0, x, 0, kk], forward[flag, 0, x, 1, kk] = real, imag
            forward[flag, 1, x, 0, kk], forward[flag, 1, x, 1, kk] = imag, -real
            inverse[flag, 0, x, 0, kk], inverse[flag, 0, x, 1, kk] = real, imag
            inverse[flag, 1, x, 0, kk], inverse[flag, 1, x, 1, kk] = imag, -real
    return narrow_type(forward.reshape(2, 64, NZ)), narrow_type(inverse.reshape(2, 64, NZ))


def frequency(i):
    return i if i < 8 else i - 16


@functools.lru_cache(None)
def y_tables():
    out = np.zeros((8, 2, 8, 16, C), np.float32)
    for n in range(8):
        for y in range(8):
            for place in range(16):
                core, par, low = place // 8, (place // 4) % 2, place % 4
                theta = angle(8 * n + y, frequency((2 * par + core) * 4 + low), NY)
                out[n, 0, y, place] = math.cos(theta) / 8.0
                out[n, 1, y, place] = math.sin(theta) / 8.0
    return out.reshape(8, 16, 512)


@functools.lru_cache(None)
def x_tables():
    forward = np.zeros((4, 8, 4, 4, 2, 2, 4, 2, 2, 2, 4), np.float32)
    inverse = np.zeros((4, 8, 4, 4, 2, 2, 4, 2, 2, 2, 4), np.float32)
    for y in range(4):
        for zl in range(8):
            for i4 in range(4):
                for y2 in range(4):
                    for c2 in range(2):
                        theta = angle(16 * y2 + 2 * zl + c2, frequency(4 * y + i4), NX)
                        co, si = math.cos(theta) / 8.0, math.sin(theta) / 8.0
                        for par in range(2):
                            for zh in range(2):
                                for k2 in range(2):
                                    kk, kind, block = 2 * zh + k2, (2 * i4 + par) % 4, 2 * zh + i4 // 2
                                    for s, t, value in ((0, 0, co), (0, 1, si), (1, 0, -si), (1, 1, co)):
                                        forward[y, zl, kind, block, s, k2, y2, c2, par, t, kk] = value
                                    for s, t, value in ((0, 0, co), (0, 1, -si), (1, 0, si), (1, 1, co)):
                                        inverse[y, zl, kind, block, t, k2, y2, c2, par, s, kk] = value
    return narrow_type(forward.reshape(32, 64, 128)), narrow_type(inverse.reshape(32, 64, 128))


def dot(a, b, dims):
    return lax.dot_general(a, b, ((dims[:1], dims[1:]), ((), ())), preferred_element_type=F32)


def gelu_parts(v):
    cumulative = 0.5 * (1.0 + lax.erf(v * (1.0 / math.sqrt(2.0))))
    bell = jnp.exp(-0.5 * v * v) * (1.0 / math.sqrt(2.0 * math.pi))
    return v * cumulative, cumulative + v * bell


def column(row, rows):
    return jnp.transpose(jnp.broadcast_to(row, (128, rows)))


def kernel(
    v_hbm, w_hbm, mix_hbm, bias_hbm, head_hbm, hb_hbm, ow_hbm, cot_hbm, ez_hbm, ei_hbm, r_hbm, t1_hbm, t2_hbm,
    pred_out, field_out, spec_out, mixg_out, headg_out,
    v_in, w_in, mix_in, bias_in, head_in, hb_in, ow_in, cot_in, ez_in, ei_in, r_rows, t1_in, t2_in, r_in,
    vf, vy, wflat, wall, wst, wcat, mixed, hidden, gp, slope, gpre, fin, lhs, srow, arow, own,
    asend, arecv, bsend, brecv, crecv, dsend, drecv,
    g1send, g1recv, g2send, g2recv, g3recv,
    in_sem, send_sem, recv_sem, passed,
):
    w = lax.axis_index("wide")
    n = lax.axis_index("narrow")
    y, zl, c = w // 16, lax.rem(w // 2, 8), lax.rem(w, 2)
    x, zh = n // 2, lax.rem(n, 2)
    q = x * 8 + y * 2 + c
    z = zh * 8 + zl
    kind, block = lax.rem(zl, 4), 2 * zh + zl // 4

    cross = []
    for dx, dy, dc in CROSS:
        x2, y2, c2 = lax.rem(x + dx, 4), lax.rem(y + dy, 4), lax.rem(c + dc, 2)
        cross.append((x2, y2, c2, (y2 * 16 + zl * 2 + c2, x2 * 2 + zh)))
    ring = []
    for d in RING:
        z2 = lax.rem(z + d, 16)
        ring.append((z2, (y * 16 + lax.rem(z2, 8) * 2 + c, x * 2 + z2 // 8)))
    near = [ring[RING.index(d)][1] for d in (14, 1, 15)]
    alike = [ring[RING.index(d)][1] for d in (8, 4, 12)]

    barrier = pltpu.get_barrier_semaphore()
    close = [where for d, (_, where) in zip(RING, ring) if min(d, 16 - d) <= 4]
    for where in close + [item[-1] for item in cross]:
        pl.semaphore_signal(barrier, inc=1, device_id=where, device_id_type=MESH)

    variant = y * 8 + zl
    loads = [
        (v_hbm, v_in), (ez_hbm, ez_in), (r_hbm.at[n], r_rows), (t1_hbm.at[variant], t1_in), (w_hbm, w_in),
        (mix_hbm, mix_in), (bias_hbm, bias_in), (head_hbm, head_in), (hb_hbm, hb_in), (ow_hbm, ow_in),
        (cot_hbm, cot_in), (ei_hbm, ei_in), (t2_hbm.at[variant], t2_in),
    ]
    loads = [pltpu.make_async_copy(a, b, in_sem.at[i]) for i, (a, b) in enumerate(loads)]
    for load in loads:
        load.start()

    def send(source, target, where, stage):
        pltpu.make_async_remote_copy(
            src_ref=source, dst_ref=target, send_sem=send_sem.at[stage], recv_sem=recv_sem.at[stage],
            device_id=where, device_id_type=MESH,
        ).start()

    def arrived(buffer, count, stage):
        part = buffer.at[pl.ds(0, count)]
        pltpu.make_async_copy(part, part, recv_sem.at[stage]).wait()

    def sent(buffer, count, stage):
        part = buffer.at[pl.ds(0, count)]
        pltpu.make_async_copy(part, part, send_sem.at[stage]).wait()

    def local_analysis(values, flag, turn):
        spectra = dot(ez_in[flag], values, (1, 1)).astype(BF)
        planes = dot(spectra[:32], r_in[:256], (1, 0)) + dot(spectra[32:], r_in[256:], (1, 0))
        for x2 in range(4):
            for c2 in range(2):
                first = planes[8 * x2 : 8 * x2 + 8, 256 * c2 : 256 * c2 + 128]
                second = planes[8 * x2 : 8 * x2 + 8, 256 * c2 + 128 : 256 * c2 + 256]
                asend[turn, x2 * 2 + c2] = jnp.concatenate([first, second], axis=0).astype(BF)
        arecv[turn, q] = asend[turn, x * 2 + c]

    def analysis_send(turn):
        for x2, y2, c2, where in cross:
            send(asend.at[turn, x2 * 2 + c2], arecv.at[turn, q], where, 4 * turn)

    def analysis_middle(turn):
        arrived(arecv.at[turn], 31, 4 * turn)
        table = t1_in[...]
        table = jnp.concatenate([table] * 4, axis=1)
        partial = dot(table, arecv[turn].reshape(512, 128), (1, 0)).astype(BF)
        for piece in range(4):
            bsend[turn, piece] = partial[16 * piece : 16 * piece + 16]
        brecv[turn, z] = bsend[turn, kind]
        for z2, where in ring:
            send(bsend.at[turn, lax.rem(z2, 4)], brecv.at[turn, z], where, 4 * turn + 1)

    def analysis_end(turn):
        arrived(brecv.at[turn], 15, 4 * turn + 1)
        total = brecv[turn, 0].astype(F32)
        for z2 in range(1, 16):
            total = total + brecv[turn, z2].astype(F32)
        for i in range(4):
            own[turn, i] = total[4 * i : 4 * i + 4]
        return total

    def paired(spectrum, low_sign, high_sign):
        for i in range(4):
            srow[4 * i : 4 * i + 2] = low_sign * spectrum[4 * i + 2 : 4 * i + 4]
            srow[4 * i + 2 : 4 * i + 4] = high_sign * spectrum[4 * i : 4 * i + 2]
        turned = srow[...]
        row = lax.broadcasted_iota(jnp.int32, (16, 128), 0)
        parts = []
        for i in range(4):
            for k2 in range(2):
                mine = (row // 4 == i) & (lax.rem(row, 2) == k2)
                parts += [jnp.where(mine, spectrum, 0.0), jnp.where(mine, turned, 0.0)]
        return jnp.concatenate(parts, axis=1).astype(BF)

    def synthesis_start(modes, turn):
        crecv[turn, kind] = modes.astype(BF)
        for where in near:
            send(crecv.at[turn, kind], crecv.at[turn, kind], where, 4 * turn + 2)

    def synthesis_middle(turn):
        arrived(crecv.at[turn], 3, 4 * turn + 2)
        planes = dot(t2_in[...], crecv[turn].reshape(64, 128), (0, 0)).astype(BF)
        for piece in range(8):
            dsend[turn, piece] = planes[16 * piece : 16 * piece + 16]
        drecv[turn, q] = dsend[turn, y * 2 + c]
        for x2, y2, c2, where in cross:
            send(dsend.at[turn, y2 * 2 + c2], drecv.at[turn, q], where, 4 * turn + 3)

    def synthesis_end(flag, turn):
        arrived(drecv.at[turn], 31, 4 * turn + 3)
        for x2 in range(4):
            for c2 in range(2):
                block = drecv[turn, x2 * 8 + c2].astype(F32)
                for y2 in range(1, 4):
                    block = block + drecv[turn, x2 * 8 + y2 * 2 + c2].astype(F32)
                lhs[8 * x2 : 8 * x2 + 8, 256 * c2 : 256 * c2 + 128] = block[:8]
                lhs[8 * x2 : 8 * x2 + 8, 256 * c2 + 128 : 256 * c2 + 256] = block[8:]
        lines = dot(lhs[...].astype(BF), r_in[...], (1, 1)).astype(BF)
        stacked = jnp.concatenate([lines[:, :256], lines[:, 256:]], axis=0)
        return dot(stacked, ei_in[flag], (0, 0))

    for i in (0, 1, 2):
        loads[i].wait()
    keep = lax.rem(lax.broadcasted_iota(jnp.int32, (32, 512), 1), 32) == lax.broadcasted_iota(jnp.int32, (32, 512), 0)
    for row in range(16):
        spread = jnp.broadcast_to(r_rows[row : row + 1], (32, 512))
        r_in[32 * row : 32 * row + 32] = jnp.where(keep, spread, 0.0).astype(BF)
    vf[...] = v_in[...].astype(F32)
    for row in range(8):
        vy[32 * row : 32 * row + 32] = vf[pl.ds(row, 32, stride=8), :].astype(BF)
    local_analysis(vy[...], 0, 0)

    for load in loads[3:]:
        load.wait()
    for j4 in range(4):
        for k2 in range(2):
            for r in range(2):
                base = 128 * (2 * k2 + r) + 32 * j4
                wflat[:, base : base + 32] = w_in[j4, k2, r]
    wall[block] = wflat[...].astype(BF)
    bias_col = column(bias_in[...], 32)
    for row in range(8):
        mixed[32 * row : 32 * row + 32] = dot(mix_in[...], vy[32 * row : 32 * row + 32], (0, 0)) + bias_col
    head_col = column(hb_in[...], 128)
    out_col = column(ow_in[...].astype(F32), 128)

    pl.semaphore_wait(barrier, len(cross) + len(close))
    for where in alike[1:]:
        pl.semaphore_signal(passed, inc=1, device_id=where, device_id_type=MESH)
    for where in alike[1:]:
        send(wall.at[block], wall.at[block], where, 11)
    analysis_send(0)
    pl.semaphore_wait(passed, 2)
    send(wall.at[block], wall.at[block], alike[0], 11)
    analysis_middle(0)
    arrived(wall, 3, 11)
    inside = lax.broadcasted_iota(jnp.int32, (128, 128), 0) // 32 == lax.broadcasted_iota(jnp.int32, (128, 128), 1) // 32
    for i in range(4):
        for part in range(4):
            compact = wall[i, :, 128 * part : 128 * part + 128].astype(F32)
            full = jnp.where(inside, jnp.concatenate([compact] * 4, axis=0), 0.0).astype(BF)
            base = 128 * (4 * i + part)
            wst[base : base + 128] = full
            wcat[:, base : base + 128] = full
    modes = dot(paired(analysis_end(0), -1.0, 1.0), wst[...], (1, 0))
    synthesis_start(modes, 0)
    synthesis_middle(0)
    pre = synthesis_end(1, 0) + mixed[...]

    value, rate = gelu_parts(pre)
    hidden[...] = value.astype(BF)
    gp[...] = rate
    for row in range(8):
        head_pre = dot(head_in[...], hidden[32 * row : 32 * row + 32], (0, 0)) + head_col
        value, rate = gelu_parts(head_pre)
        pred_out[row : row + 1] = dot(ow_in[...], value.astype(BF), (1, 0))
        slope[128 * row : 128 * row + 128] = (cot_in[row : row + 1] * out_col * rate).astype(BF)
        back = dot(head_in[...], slope[128 * row : 128 * row + 128], (1, 0))
        gpre[32 * row : 32 * row + 32] = (back * gp[32 * row : 32 * row + 32]).astype(BF)
    local_analysis(gpre[...], 1, 1)
    analysis_send(1)

    head_grad = jnp.zeros((32, 128), F32)
    mix_grad = jnp.zeros((32, 32), F32)
    for row in range(8):
        head_grad = head_grad + dot(hidden[32 * row : 32 * row + 32], slope[128 * row : 128 * row + 128], (1, 1))
        mix_grad = mix_grad + dot(vy[32 * row : 32 * row + 32], gpre[32 * row : 32 * row + 32], (1, 1))
    folded = jnp.concatenate([mix_grad[8 * i : 8 * i + 8] for i in range(4)], axis=1)
    for i in range(16):
        g1send[i] = head_grad[2 * i : 2 * i + 2]
    for i in range(4):
        g1send[16 + i] = folded[2 * i : 2 * i + 2]
    for i in range(20, 32):
        g1send[i] = jnp.zeros((2, 128), F32)
    g1recv[q] = g1send[q]
    for x2, y2, c2, where in cross:
        send(g1send.at[x2 * 8 + y2 * 2 + c2], g1recv.at[q], where, 8)
    for row in range(8):
        mixed[32 * row : 32 * row + 32] = dot(mix_in[...], gpre[32 * row : 32 * row + 32], (1, 0))

    analysis_middle(1)

    arrived(g1recv, 31, 8)
    total = g1recv[0]
    for i in range(1, 32):
        total = total + g1recv[i]
    g2send[...] = total
    g2recv[z] = total
    for z2, where in ring:
        send(g2send, g2recv.at[z], where, 9)

    modes = dot(paired(analysis_end(1), 1.0, -1.0), wcat[...], (1, 1))
    synthesis_start(modes, 1)
    spectrum = own[0, block]
    adjoint = own[1, block]

    arrived(g2recv, 15, 9)
    total = g2recv[0]
    for i in range(1, 16):
        total = total + g2recv[i]
    g3recv[q] = total
    for x2, y2, c2, where in cross:
        send(g3recv.at[q], g3recv.at[q], where, 10)

    for j4 in range(4):
        arow[4 * j4 : 4 * j4 + 4] = adjoint[:, 32 * j4 : 32 * j4 + 32]
    rows = lax.broadcasted_iota(jnp.int32, (16, 128), 0)
    lanes = lax.broadcasted_iota(jnp.int32, (16, 128), 1)
    diagonal = rows // 4 == lanes // 32
    targets = arow[...].astype(BF)
    part = lax.rem(rows, 4)
    for k2 in range(2):
        real = jnp.broadcast_to(spectrum[k2 : k2 + 1], (16, 128))
        imag = jnp.broadcast_to(spectrum[2 + k2 : 3 + k2], (16, 128))
        for r in range(2):
            on_real = real if r == 0 else -imag
            on_imag = imag if r == 0 else real
            left = jnp.where(part == k2, on_real, jnp.where(part == 2 + k2, on_imag, 0.0))
            left = jnp.where(diagonal, left, 0.0).astype(BF)
            product = dot(left, targets, (0, 0))
            for j4 in range(4):
                spec_out[j4, k2, r] = product[32 * j4 : 32 * j4 + 32]

    synthesis_middle(1)

    arrived(g3recv, 31, 10)
    for i in range(16):
        headg_out[2 * i : 2 * i + 2] = g3recv[i]
    for i in range(4):
        rows2 = g3recv[16 + i]
        for j in range(4):
            mixg_out[8 * j + 2 * i : 8 * j + 2 * i + 2] = rows2[:, 32 * j : 32 * j + 32]

    field = synthesis_end(0, 1) + mixed[...]
    for row in range(8):
        fin[pl.ds(row, 32, stride=8), :] = field[32 * row : 32 * row + 32]
    field_out[...] = fin[...].astype(BF)

    for turn in range(2):
        sent(arecv.at[turn], 31, 4 * turn)
        sent(brecv.at[turn], 15, 4 * turn + 1)
        sent(crecv.at[turn], 3, 4 * turn + 2)
        sent(drecv.at[turn], 31, 4 * turn + 3)
    sent(g1recv, 31, 8)
    sent(g2recv, 15, 9)
    sent(g3recv, 31, 10)
    sent(wall, 3, 11)


def publish(*refs):
    sem = refs[-1]
    copies = [pltpu.make_async_copy(refs[i], refs[5 + i], sem.at[i]) for i in (2, 1, 0, 3, 4)]
    for copy in copies:
        copy.start()
    for copy in copies:
        copy.wait()


def body(lifted_field, spectral_weight, mix_weight, mix_bias, head_weight, head_bias, out_weight, cotangent):
    forward_z, inverse_z = z_tables()
    forward_x, inverse_x = x_tables()
    inputs = (
        lifted_field.reshape(256, 128), spectral_weight, mix_weight, mix_bias.reshape(1, 32), head_weight,
        head_bias.reshape(1, 128), out_weight.reshape(1, 128), cotangent.reshape(8, 128),
        jnp.asarray(forward_z), jnp.asarray(inverse_z), jnp.asarray(y_tables()), jnp.asarray(forward_x), jnp.asarray(inverse_x),
    )
    inputs = tuple(pltpu.with_memory_space_constraint(a, pltpu.HBM) for a in inputs)
    whole = lambda a: pltpu.VMEM(a.shape, a.dtype)
    tail = lambda a: pltpu.VMEM(a.shape[1:], a.dtype)
    outputs = [
        jax.ShapeDtypeStruct((8, 128), F32), jax.ShapeDtypeStruct((256, 128), BF),
        jax.ShapeDtypeStruct((4, 2, 2, 32, 32), F32), jax.ShapeDtypeStruct((32, 32), F32), jax.ShapeDtypeStruct((32, 128), F32),
    ]
    scratch = [whole(a) for a in inputs[:10]] + [tail(a) for a in inputs[10:]] + [pltpu.VMEM((512, 512), BF)]
    scratch += [
        pltpu.VMEM((256, 128), F32), pltpu.VMEM((256, 128), BF), pltpu.VMEM((32, 512), F32), pltpu.VMEM((4, 32, 512), BF),
        pltpu.VMEM((2048, 128), BF), pltpu.VMEM((128, 2048), BF),
        pltpu.VMEM((256, 128), F32), pltpu.VMEM((256, 128), BF), pltpu.VMEM((256, 128), F32), pltpu.VMEM((1024, 128), BF),
        pltpu.VMEM((256, 128), BF), pltpu.VMEM((256, 128), F32), pltpu.VMEM((32, 512), F32),
        pltpu.VMEM((16, 128), F32), pltpu.VMEM((16, 32), F32), pltpu.VMEM((2, 4, 4, 128), F32),
    ]
    scratch += [
        pltpu.VMEM((2, 8, 16, 128), BF), pltpu.VMEM((2, 32, 16, 128), BF),
        pltpu.VMEM((2, 4, 16, 128), BF), pltpu.VMEM((2, 16, 16, 128), BF), pltpu.VMEM((2, 4, 16, 128), BF),
        pltpu.VMEM((2, 8, 16, 128), BF), pltpu.VMEM((2, 32, 16, 128), BF),
        pltpu.VMEM((32, 2, 128), F32), pltpu.VMEM((32, 2, 128), F32),
        pltpu.VMEM((2, 128), F32), pltpu.VMEM((16, 2, 128), F32), pltpu.VMEM((32, 2, 128), F32),
        pltpu.SemaphoreType.DMA((13,)), pltpu.SemaphoreType.DMA((12,)), pltpu.SemaphoreType.DMA((12,)), pltpu.SemaphoreType.REGULAR,
    ]
    results = pl.pallas_call(
        kernel,
        out_shape=outputs,
        in_specs=[pl.BlockSpec(memory_space=pltpu.HBM)] * len(inputs),
        out_specs=[pl.BlockSpec(memory_space=pltpu.VMEM)] * len(outputs),
        scratch_shapes=scratch,
        name="step",
        compiler_params=pltpu.CompilerParams(collective_id=0, has_side_effects=True, vmem_limit_bytes=32 << 20),
    )(*inputs)
    prediction, field, spectral, mix_grad, head_grad = pl.pallas_call(
        publish,
        out_shape=outputs,
        in_specs=[pl.BlockSpec(memory_space=pltpu.VMEM)] * len(outputs),
        out_specs=[pl.BlockSpec(memory_space=pltpu.HBM)] * len(outputs),
        scratch_shapes=[pltpu.SemaphoreType.DMA((5,))],
        name="publish",
        compiler_params=pltpu.CompilerParams(vmem_limit_bytes=4 << 20),
    )(*results)
    return prediction.reshape(1, 8, 128), field.reshape(1, 32, 8, 128), spectral, mix_grad, head_grad


def solution(mesh):
    return jax.shard_map(
        body,
        mesh=mesh,
        in_specs=(
            P("wide", None, "narrow", None),
            P("wide", "narrow", None, None, None),
            P(),
            P(),
            P(),
            P(),
            P(),
            P("wide", "narrow", None),
        ),
        out_specs=(
            P("wide", "narrow", None),
            P("wide", None, "narrow", None),
            P("wide", "narrow", None, None, None),
            P(),
            P(),
        ),
        check_vma=False,
    )
```

```python
import functools
import math

import jax
import jax.numpy as jnp
import ml_dtypes
import numpy as np
from jax import lax
from jax.experimental import pallas as pl
from jax.experimental.pallas import tpu as pltpu
from jax.sharding import PartitionSpec as P

MESH = pl.DeviceIdType.MESH
BF = jnp.bfloat16
F32 = jnp.float32
NX, NY, NZ, C, HID = 64, 64, 128, 32, 128
CROSS = [(dx, dy, dc) for dx in range(4) for dy in range(4) for dc in range(2) if dx or dy or dc]
CROSS.sort(key=lambda t: (-(min(t[0], 4 - t[0]) + min(t[1], 4 - t[1])), t))
RING = sorted(range(1, 16), key=lambda d: (-min(d, 16 - d), d))


def angle(position, frequency, length):
    return 2.0 * math.pi * ((position * frequency) % length) / length


def narrow_type(table):
    return np.asarray(table, np.float32).astype(ml_dtypes.bfloat16)


@functools.lru_cache(None)
def z_tables():
    forward = np.zeros((2, 2, 4, 2, 4, NZ))
    inverse = np.zeros((2, 2, 4, 2, 4, NZ))
    z = np.arange(NZ)
    for flag in range(2):
        for k in range(16):
            scale = (2.0 if flag and k else 1.0) / math.sqrt(NZ)
            real, imag = scale * np.cos(angle(z, k, NZ)), -scale * np.sin(angle(z, k, NZ))
            x, kk = k // 4, k % 4
            forward[flag, 0, x, 0, kk], forward[flag, 0, x, 1, kk] = real, imag
            forward[flag, 1, x, 0, kk], forward[flag, 1, x, 1, kk] = imag, -real
            inverse[flag, 0, x, 0, kk], inverse[flag, 0, x, 1, kk] = real, imag
            inverse[flag, 1, x, 0, kk], inverse[flag, 1, x, 1, kk] = imag, -real
    return narrow_type(forward.reshape(2, 64, NZ)), narrow_type(inverse.reshape(2, 64, NZ))


def frequency(i):
    return i if i < 8 else i - 16


@functools.lru_cache(None)
def y_tables():
    out = np.zeros((8, 2, 8, 16, C), np.float32)
    for n in range(8):
        for y in range(8):
            for place in range(16):
                core, par, low = place // 8, (place // 4) % 2, place % 4
                theta = angle(8 * n + y, frequency((2 * par + core) * 4 + low), NY)
                out[n, 0, y, place] = math.cos(theta) / 8.0
                out[n, 1, y, place] = math.sin(theta) / 8.0
    return out.reshape(8, 16, 512)


@functools.lru_cache(None)
def x_tables():
    forward = np.zeros((4, 8, 4, 4, 2, 2, 4, 2, 2, 2, 4), np.float32)
    inverse = np.zeros((4, 8, 4, 4, 2, 2, 4, 2, 2, 2, 4), np.float32)
    for y in range(4):
        for zl in range(8):
            for i4 in range(4):
                for y2 in range(4):
                    for c2 in range(2):
                        theta = angle(16 * y2 + 2 * zl + c2, frequency(4 * y + i4), NX)
                        co, si = math.cos(theta) / 8.0, math.sin(theta) / 8.0
                        for par in range(2):
                            for zh in range(2):
                                for k2 in range(2):
                                    kk, kind, block = 2 * zh + k2, (2 * i4 + par) % 4, 2 * zh + i4 // 2
                                    for s, t, value in ((0, 0, co), (0, 1, si), (1, 0, -si), (1, 1, co)):
                                        forward[y, zl, kind, block, s, k2, y2, c2, par, t, kk] = value
                                    for s, t, value in ((0, 0, co), (0, 1, -si), (1, 0, si), (1, 1, co)):
                                        inverse[y, zl, kind, block, t, k2, y2, c2, par, s, kk] = value
    return narrow_type(forward.reshape(32, 64, 128)), narrow_type(inverse.reshape(32, 64, 128))


def dot(a, b, dims):
    return lax.dot_general(a, b, ((dims[:1], dims[1:]), ((), ())), preferred_element_type=F32)


def gelu_parts(v):
    cumulative = 0.5 * (1.0 + lax.erf(v * (1.0 / math.sqrt(2.0))))
    bell = jnp.exp(-0.5 * v * v) * (1.0 / math.sqrt(2.0 * math.pi))
    return v * cumulative, cumulative + v * bell


def column(row, rows):
    return jnp.transpose(jnp.broadcast_to(row, (128, rows)))


def kernel(
    v_hbm, w_hbm, mix_hbm, bias_hbm, head_hbm, hb_hbm, ow_hbm, cot_hbm, ez_hbm, ei_hbm, r_hbm, t1_hbm, t2_hbm,
    pred_out, field_out, spec_out, mixg_out, headg_out,
    v_in, w_in, mix_in, bias_in, head_in, hb_in, ow_in, cot_in, ez_in, ei_in, r_rows, t1_in, t2_in, r_in,
    vf, vy, wflat, wall, wst, wcat, mixed, hidden, gp, slope, gpre, fin, lhs, srow, arow, own,
    asend, arecv, bsend, brecv, crecv, dsend, drecv,
    g1send, g1recv, g2send, g2recv, g3recv,
    in_sem, send_sem, recv_sem, passed,
):
    w = lax.axis_index("wide")
    n = lax.axis_index("narrow")
    y, zl, c = w // 16, lax.rem(w // 2, 8), lax.rem(w, 2)
    x, zh = n // 2, lax.rem(n, 2)
    q = x * 8 + y * 2 + c
    z = zh * 8 + zl
    kind, block = lax.rem(zl, 4), 2 * zh + zl // 4

    cross = []
    for dx, dy, dc in CROSS:
        x2, y2, c2 = lax.rem(x + dx, 4), lax.rem(y + dy, 4), lax.rem(c + dc, 2)
        cross.append((x2, y2, c2, (y2 * 16 + zl * 2 + c2, x2 * 2 + zh)))
    ring = []
    for d in RING:
        z2 = lax.rem(z + d, 16)
        ring.append((z2, (y * 16 + lax.rem(z2, 8) * 2 + c, x * 2 + z2 // 8)))
    near = [ring[RING.index(d)][1] for d in (14, 1, 15)]
    alike = [ring[RING.index(d)][1] for d in (8, 4, 12)]

    barrier = pltpu.get_barrier_semaphore()
    close = [where for d, (_, where) in zip(RING, ring) if min(d, 16 - d) <= 4]
    for where in close + [item[-1] for item in cross]:
        pl.semaphore_signal(barrier, inc=1, device_id=where, device_id_type=MESH)

    variant = y * 8 + zl
    loads = [
        (v_hbm, v_in), (ez_hbm, ez_in), (r_hbm.at[n], r_rows), (t1_hbm.at[variant], t1_in), (w_hbm, w_in),
        (mix_hbm, mix_in), (bias_hbm, bias_in), (head_hbm, head_in), (hb_hbm, hb_in), (ow_hbm, ow_in),
        (cot_hbm, cot_in), (ei_hbm, ei_in), (t2_hbm.at[variant], t2_in),
    ]
    loads = [pltpu.make_async_copy(a, b, in_sem.at[i]) for i, (a, b) in enumerate(loads)]
    for load in loads:
        load.start()

    def send(source, target, where, stage):
        pltpu.make_async_remote_copy(
            src_ref=source, dst_ref=target, send_sem=send_sem.at[stage], recv_sem=recv_sem.at[stage],
            device_id=where, device_id_type=MESH,
        ).start()

    def arrived(buffer, count, stage):
        part = buffer.at[pl.ds(0, count)]
        pltpu.make_async_copy(part, part, recv_sem.at[stage]).wait()

    def sent(buffer, count, stage):
        part = buffer.at[pl.ds(0, count)]
        pltpu.make_async_copy(part, part, send_sem.at[stage]).wait()

    def local_analysis(values, flag, turn):
        spectra = dot(ez_in[flag], values, (1, 1)).astype(BF)
        planes = dot(spectra[:32], r_in[:256], (1, 0)) + dot(spectra[32:], r_in[256:], (1, 0))
        for x2 in range(4):
            for c2 in range(2):
                first = planes[8 * x2 : 8 * x2 + 8, 256 * c2 : 256 * c2 + 128]
                second = planes[8 * x2 : 8 * x2 + 8, 256 * c2 + 128 : 256 * c2 + 256]
                asend[turn, x2 * 2 + c2] = jnp.concatenate([first, second], axis=0).astype(BF)
        arecv[turn, q] = asend[turn, x * 2 + c]

    def analysis_send(turn):
        for x2, y2, c2, where in cross:
            send(asend.at[turn, x2 * 2 + c2], arecv.at[turn, q], where, 4 * turn)

    def analysis_middle(turn):
        arrived(arecv.at[turn], 31, 4 * turn)
        table = t1_in[...]
        table = jnp.concatenate([table] * 4, axis=1)
        partial = dot(table, arecv[turn].reshape(512, 128), (1, 0)).astype(BF)
        for piece in range(4):
            bsend[turn, piece] = partial[16 * piece : 16 * piece + 16]
        brecv[turn, z] = bsend[turn, kind]
        for z2, where in ring:
            send(bsend.at[turn, lax.rem(z2, 4)], brecv.at[turn, z], where, 4 * turn + 1)

    def analysis_end(turn):
        arrived(brecv.at[turn], 15, 4 * turn + 1)
        total = brecv[turn, 0].astype(F32)
        for z2 in range(1, 16):
            total = total + brecv[turn, z2].astype(F32)
        for i in range(4):
            own[turn, i] = total[4 * i : 4 * i + 4]
        return total

    def paired(spectrum, low_sign, high_sign):
        for i in range(4):
            srow[4 * i : 4 * i + 2] = low_sign * spectrum[4 * i + 2 : 4 * i + 4]
            srow[4 * i + 2 : 4 * i + 4] = high_sign * spectrum[4 * i : 4 * i + 2]
        turned = srow[...]
        row = lax.broadcasted_iota(jnp.int32, (16, 128), 0)
        parts = []
        for i in range(4):
            for k2 in range(2):
                mine = (row // 4 == i) & (lax.rem(row, 2) == k2)
                parts += [jnp.where(mine, spectrum, 0.0), jnp.where(mine, turned, 0.0)]
        return jnp.concatenate(parts, axis=1).astype(BF)

    def synthesis_start(modes, turn):
        crecv[turn, kind] = modes.astype(BF)
        for where in near:
            send(crecv.at[turn, kind], crecv.at[turn, kind], where, 4 * turn + 2)

    def synthesis_middle(turn):
        arrived(crecv.at[turn], 3, 4 * turn + 2)
        planes = dot(t2_in[...], crecv[turn].reshape(64, 128), (0, 0)).astype(BF)
        for piece in range(8):
            dsend[turn, piece] = planes[16 * piece : 16 * piece + 16]
        drecv[turn, q] = dsend[turn, y * 2 + c]
        for x2, y2, c2, where in cross:
            send(dsend.at[turn, y2 * 2 + c2], drecv.at[turn, q], where, 4 * turn + 3)

    def synthesis_end(flag, turn):
        arrived(drecv.at[turn], 31, 4 * turn + 3)
        for x2 in range(4):
            for c2 in range(2):
                block = drecv[turn, x2 * 8 + c2].astype(F32)
                for y2 in range(1, 4):
                    block = block + drecv[turn, x2 * 8 + y2 * 2 + c2].astype(F32)
                lhs[8 * x2 : 8 * x2 + 8, 256 * c2 : 256 * c2 + 128] = block[:8]
                lhs[8 * x2 : 8 * x2 + 8, 256 * c2 + 128 : 256 * c2 + 256] = block[8:]
        lines = dot(lhs[...].astype(BF), r_in[...], (1, 1)).astype(BF)
        stacked = jnp.concatenate([lines[:, :256], lines[:, 256:]], axis=0)
        return dot(stacked, ei_in[flag], (0, 0))

    for i in (0, 1, 2):
        loads[i].wait()
    keep = lax.rem(lax.broadcasted_iota(jnp.int32, (32, 512), 1), 32) == lax.broadcasted_iota(jnp.int32, (32, 512), 0)
    for row in range(16):
        spread = jnp.broadcast_to(r_rows[row : row + 1], (32, 512))
        r_in[32 * row : 32 * row + 32] = jnp.where(keep, spread, 0.0).astype(BF)
    vf[...] = v_in[...].astype(F32)
    for row in range(8):
        vy[32 * row : 32 * row + 32] = vf[pl.ds(row, 32, stride=8), :].astype(BF)
    local_analysis(vy[...], 0, 0)

    for load in loads[3:]:
        load.wait()
    for j4 in range(4):
        for k2 in range(2):
            for r in range(2):
                base = 128 * (2 * k2 + r) + 32 * j4
                wflat[:, base : base + 32] = w_in[j4, k2, r]
    wall[block] = wflat[...].astype(BF)
    bias_col = column(bias_in[...], 32)
    for row in range(8):
        mixed[32 * row : 32 * row + 32] = dot(mix_in[...], vy[32 * row : 32 * row + 32], (0, 0)) + bias_col
    head_col = column(hb_in[...], 128)
    out_col = column(ow_in[...].astype(F32), 128)

    pl.semaphore_wait(barrier, len(cross) + len(close))
    for where in alike[1:]:
        pl.semaphore_signal(passed, inc=1, device_id=where, device_id_type=MESH)
    for where in alike[1:]:
        send(wall.at[block], wall.at[block], where, 11)
    analysis_send(0)
    pl.semaphore_wait(passed, 2)
    send(wall.at[block], wall.at[block], alike[0], 11)
    analysis_middle(0)
    arrived(wall, 3, 11)
    inside = lax.broadcasted_iota(jnp.int32, (128, 128), 0) // 32 == lax.broadcasted_iota(jnp.int32, (128, 128), 1) // 32
    for i in range(4):
        for part in range(4):
            compact = wall[i, :, 128 * part : 128 * part + 128].astype(F32)
            full = jnp.where(inside, jnp.concatenate([compact] * 4, axis=0), 0.0).astype(BF)
            base = 128 * (4 * i + part)
            wst[base : base + 128] = full
            wcat[:, base : base + 128] = full
    modes = dot(paired(analysis_end(0), -1.0, 1.0), wst[...], (1, 0))
    synthesis_start(modes, 0)
    synthesis_middle(0)
    pre = synthesis_end(1, 0) + mixed[...]

    value, rate = gelu_parts(pre)
    hidden[...] = value.astype(BF)
    gp[...] = rate
    for first in range(0, 8, 2):
        group = range(first, first + 2)
        side = jnp.concatenate([hidden[32 * row : 32 * row + 32] for row in group], axis=1)
        head_pre = dot(head_in[...], side, (0, 0)) + jnp.concatenate([head_col] * 2, axis=1)
        value, rate = gelu_parts(head_pre)
        line = dot(ow_in[...], value.astype(BF), (1, 0))
        drive = jnp.concatenate([cot_in[row : row + 1] * out_col for row in group], axis=1)
        tilt = (drive * rate).astype(BF)
        back = dot(head_in[...], tilt, (1, 0))
        for i, row in enumerate(group):
            lanes = slice(128 * i, 128 * i + 128)
            pred_out[row : row + 1] = line[:, lanes]
            slope[128 * row : 128 * row + 128] = tilt[:, lanes]
            gpre[32 * row : 32 * row + 32] = (back[:, lanes] * gp[32 * row : 32 * row + 32]).astype(BF)
    local_analysis(gpre[...], 1, 1)
    analysis_send(1)

    head_grad = jnp.zeros((32, 128), F32)
    mix_grad = jnp.zeros((32, 32), F32)
    for row in range(8):
        head_grad = head_grad + dot(hidden[32 * row : 32 * row + 32], slope[128 * row : 128 * row + 128], (1, 1))
        mix_grad = mix_grad + dot(vy[32 * row : 32 * row + 32], gpre[32 * row : 32 * row + 32], (1, 1))
    folded = jnp.concatenate([mix_grad[8 * i : 8 * i + 8] for i in range(4)], axis=1)
    for i in range(16):
        g1send[i] = head_grad[2 * i : 2 * i + 2]
    for i in range(4):
        g1send[16 + i] = folded[2 * i : 2 * i + 2]
    for i in range(20, 32):
        g1send[i] = jnp.zeros((2, 128), F32)
    g1recv[q] = g1send[q]
    for x2, y2, c2, where in cross:
        send(g1send.at[x2 * 8 + y2 * 2 + c2], g1recv.at[q], where, 8)
    for row in range(8):
        mixed[32 * row : 32 * row + 32] = dot(mix_in[...], gpre[32 * row : 32 * row + 32], (1, 0))

    analysis_middle(1)

    arrived(g1recv, 31, 8)
    total = g1recv[0]
    for i in range(1, 32):
        total = total + g1recv[i]
    g2send[...] = total
    g2recv[z] = total
    for z2, where in ring:
        send(g2send, g2recv.at[z], where, 9)

    modes = dot(paired(analysis_end(1), 1.0, -1.0), wcat[...], (1, 1))
    synthesis_start(modes, 1)
    spectrum = own[0, block]
    adjoint = own[1, block]

    arrived(g2recv, 15, 9)
    total = g2recv[0]
    for i in range(1, 16):
        total = total + g2recv[i]
    g3recv[q] = total
    for x2, y2, c2, where in cross:
        send(g3recv.at[q], g3recv.at[q], where, 10)

    synthesis_middle(1)

    for j4 in range(4):
        arow[4 * j4 : 4 * j4 + 4] = adjoint[:, 32 * j4 : 32 * j4 + 32]
    rows = lax.broadcasted_iota(jnp.int32, (16, 128), 0)
    lanes = lax.broadcasted_iota(jnp.int32, (16, 128), 1)
    diagonal = rows // 4 == lanes // 32
    targets = arow[...].astype(BF)
    part = lax.rem(rows, 4)
    for k2 in range(2):
        real = jnp.broadcast_to(spectrum[k2 : k2 + 1], (16, 128))
        imag = jnp.broadcast_to(spectrum[2 + k2 : 3 + k2], (16, 128))
        for r in range(2):
            on_real = real if r == 0 else -imag
            on_imag = imag if r == 0 else real
            left = jnp.where(part == k2, on_real, jnp.where(part == 2 + k2, on_imag, 0.0))
            left = jnp.where(diagonal, left, 0.0).astype(BF)
            product = dot(left, targets, (0, 0))
            for j4 in range(4):
                spec_out[j4, k2, r] = product[32 * j4 : 32 * j4 + 32]

    arrived(g3recv, 31, 10)
    for i in range(16):
        headg_out[2 * i : 2 * i + 2] = g3recv[i]
    for i in range(4):
        rows2 = g3recv[16 + i]
        for j in range(4):
            mixg_out[8 * j + 2 * i : 8 * j + 2 * i + 2] = rows2[:, 32 * j : 32 * j + 32]

    field = synthesis_end(0, 1) + mixed[...]
    for row in range(8):
        fin[pl.ds(row, 32, stride=8), :] = field[32 * row : 32 * row + 32]
    field_out[...] = fin[...].astype(BF)

    for turn in range(2):
        sent(arecv.at[turn], 31, 4 * turn)
        sent(brecv.at[turn], 15, 4 * turn + 1)
        sent(crecv.at[turn], 3, 4 * turn + 2)
        sent(drecv.at[turn], 31, 4 * turn + 3)
    sent(g1recv, 31, 8)
    sent(g2recv, 15, 9)
    sent(g3recv, 31, 10)
    sent(wall, 3, 11)


def publish(*refs):
    sem = refs[-1]
    copies = [pltpu.make_async_copy(refs[i], refs[5 + i], sem.at[i]) for i in (2, 1, 0, 3, 4)]
    for copy in copies:
        copy.start()
    for copy in copies:
        copy.wait()


def body(lifted_field, spectral_weight, mix_weight, mix_bias, head_weight, head_bias, out_weight, cotangent):
    forward_z, inverse_z = z_tables()
    forward_x, inverse_x = x_tables()
    inputs = (
        lifted_field.reshape(256, 128), spectral_weight, mix_weight, mix_bias.reshape(1, 32), head_weight,
        head_bias.reshape(1, 128), out_weight.reshape(1, 128), cotangent.reshape(8, 128),
        jnp.asarray(forward_z), jnp.asarray(inverse_z), jnp.asarray(y_tables()), jnp.asarray(forward_x), jnp.asarray(inverse_x),
    )
    inputs = tuple(pltpu.with_memory_space_constraint(a, pltpu.HBM) for a in inputs)
    whole = lambda a: pltpu.VMEM(a.shape, a.dtype)
    tail = lambda a: pltpu.VMEM(a.shape[1:], a.dtype)
    outputs = [
        jax.ShapeDtypeStruct((8, 128), F32), jax.ShapeDtypeStruct((256, 128), BF),
        jax.ShapeDtypeStruct((4, 2, 2, 32, 32), F32), jax.ShapeDtypeStruct((32, 32), F32), jax.ShapeDtypeStruct((32, 128), F32),
    ]
    scratch = [whole(a) for a in inputs[:10]] + [tail(a) for a in inputs[10:]] + [pltpu.VMEM((512, 512), BF)]
    scratch += [
        pltpu.VMEM((256, 128), F32), pltpu.VMEM((256, 128), BF), pltpu.VMEM((32, 512), F32), pltpu.VMEM((4, 32, 512), BF),
        pltpu.VMEM((2048, 128), BF), pltpu.VMEM((128, 2048), BF),
        pltpu.VMEM((256, 128), F32), pltpu.VMEM((256, 128), BF), pltpu.VMEM((256, 128), F32), pltpu.VMEM((1024, 128), BF),
        pltpu.VMEM((256, 128), BF), pltpu.VMEM((256, 128), F32), pltpu.VMEM((32, 512), F32),
        pltpu.VMEM((16, 128), F32), pltpu.VMEM((16, 32), F32), pltpu.VMEM((2, 4, 4, 128), F32),
    ]
    scratch += [
        pltpu.VMEM((2, 8, 16, 128), BF), pltpu.VMEM((2, 32, 16, 128), BF),
        pltpu.VMEM((2, 4, 16, 128), BF), pltpu.VMEM((2, 16, 16, 128), BF), pltpu.VMEM((2, 4, 16, 128), BF),
        pltpu.VMEM((2, 8, 16, 128), BF), pltpu.VMEM((2, 32, 16, 128), BF),
        pltpu.VMEM((32, 2, 128), F32), pltpu.VMEM((32, 2, 128), F32),
        pltpu.VMEM((2, 128), F32), pltpu.VMEM((16, 2, 128), F32), pltpu.VMEM((32, 2, 128), F32),
        pltpu.SemaphoreType.DMA((13,)), pltpu.SemaphoreType.DMA((12,)), pltpu.SemaphoreType.DMA((12,)), pltpu.SemaphoreType.REGULAR,
    ]
    results = pl.pallas_call(
        kernel,
        out_shape=outputs,
        in_specs=[pl.BlockSpec(memory_space=pltpu.HBM)] * len(inputs),
        out_specs=[pl.BlockSpec(memory_space=pltpu.VMEM)] * len(outputs),
        scratch_shapes=scratch,
        name="step",
        compiler_params=pltpu.CompilerParams(collective_id=0, has_side_effects=True, vmem_limit_bytes=32 << 20),
    )(*inputs)
    prediction, field, spectral, mix_grad, head_grad = pl.pallas_call(
        publish,
        out_shape=outputs,
        in_specs=[pl.BlockSpec(memory_space=pltpu.VMEM)] * len(outputs),
        out_specs=[pl.BlockSpec(memory_space=pltpu.HBM)] * len(outputs),
        scratch_shapes=[pltpu.SemaphoreType.DMA((5,))],
        name="publish",
        compiler_params=pltpu.CompilerParams(vmem_limit_bytes=4 << 20),
    )(*results)
    return prediction.reshape(1, 8, 128), field.reshape(1, 32, 8, 128), spectral, mix_grad, head_grad


def solution(mesh):
    return jax.shard_map(
        body,
        mesh=mesh,
        in_specs=(
            P("wide", None, "narrow", None),
            P("wide", "narrow", None, None, None),
            P(),
            P(),
            P(),
            P(),
            P(),
            P("wide", "narrow", None),
        ),
        out_specs=(
            P("wide", "narrow", None),
            P("wide", None, "narrow", None),
            P("wide", "narrow", None, None, None),
            P(),
            P(),
        ),
        check_vma=False,
    )
```

```python
import functools
import math

import jax
import jax.numpy as jnp
import ml_dtypes
import numpy as np
from jax import lax
from jax.experimental import pallas as pl
from jax.experimental.pallas import tpu as pltpu
from jax.sharding import PartitionSpec as P

MESH = pl.DeviceIdType.MESH
BF = jnp.bfloat16
F32 = jnp.float32
NX, NY, NZ, C, HID = 64, 64, 128, 32, 128
CROSS = [(dx, dy, dc) for dx in range(4) for dy in range(4) for dc in range(2) if dx or dy or dc]
CROSS.sort(key=lambda t: (-(min(t[0], 4 - t[0]) + min(t[1], 4 - t[1])), t))
RING = sorted(range(1, 16), key=lambda d: (-min(d, 16 - d), d))


def angle(position, frequency, length):
    return 2.0 * math.pi * ((position * frequency) % length) / length


def narrow_type(table):
    return np.asarray(table, np.float32).astype(ml_dtypes.bfloat16)


@functools.lru_cache(None)
def z_tables():
    forward = np.zeros((2, 2, 4, 2, 4, NZ))
    inverse = np.zeros((2, 2, 4, 2, 4, NZ))
    z = np.arange(NZ)
    for flag in range(2):
        for k in range(16):
            scale = (2.0 if flag and k else 1.0) / math.sqrt(NZ)
            real, imag = scale * np.cos(angle(z, k, NZ)), -scale * np.sin(angle(z, k, NZ))
            x, kk = k // 4, k % 4
            forward[flag, 0, x, 0, kk], forward[flag, 0, x, 1, kk] = real, imag
            forward[flag, 1, x, 0, kk], forward[flag, 1, x, 1, kk] = imag, -real
            inverse[flag, 0, x, 0, kk], inverse[flag, 0, x, 1, kk] = real, imag
            inverse[flag, 1, x, 0, kk], inverse[flag, 1, x, 1, kk] = imag, -real
    return narrow_type(forward.reshape(2, 64, NZ)), narrow_type(inverse.reshape(2, 64, NZ))


def frequency(i):
    return i if i < 8 else i - 16


@functools.lru_cache(None)
def y_tables():
    out = np.zeros((8, 2, 8, 16, C), np.float32)
    for n in range(8):
        for y in range(8):
            for place in range(16):
                core, par, low = place // 8, (place // 4) % 2, place % 4
                theta = angle(8 * n + y, frequency((2 * par + core) * 4 + low), NY)
                out[n, 0, y, place] = math.cos(theta) / 8.0
                out[n, 1, y, place] = math.sin(theta) / 8.0
    return out.reshape(8, 16, 512)


@functools.lru_cache(None)
def x_tables():
    forward = np.zeros((4, 8, 4, 4, 2, 2, 4, 2, 2, 2, 4), np.float32)
    inverse = np.zeros((4, 8, 4, 4, 2, 2, 4, 2, 2, 2, 4), np.float32)
    for y in range(4):
        for zl in range(8):
            for i4 in range(4):
                for y2 in range(4):
                    for c2 in range(2):
                        theta = angle(16 * y2 + 2 * zl + c2, frequency(4 * y + i4), NX)
                        co, si = math.cos(theta) / 8.0, math.sin(theta) / 8.0
                        for par in range(2):
                            for zh in range(2):
                                for k2 in range(2):
                                    kk, kind, block = 2 * zh + k2, (2 * i4 + par) % 4, 2 * zh + i4 // 2
                                    for s, t, value in ((0, 0, co), (0, 1, si), (1, 0, -si), (1, 1, co)):
                                        forward[y, zl, kind, block, s, k2, y2, c2, par, t, kk] = value
                                    for s, t, value in ((0, 0, co), (0, 1, -si), (1, 0, si), (1, 1, co)):
                                        inverse[y, zl, kind, block, t, k2, y2, c2, par, s, kk] = value
    return narrow_type(forward.reshape(32, 64, 128)), narrow_type(inverse.reshape(32, 64, 128))


def dot(a, b, dims):
    return lax.dot_general(a, b, ((dims[:1], dims[1:]), ((), ())), preferred_element_type=F32)


def gelu_parts(v):
    cumulative = 0.5 * (1.0 + lax.erf(v * (1.0 / math.sqrt(2.0))))
    bell = jnp.exp(-0.5 * v * v) * (1.0 / math.sqrt(2.0 * math.pi))
    return v * cumulative, cumulative + v * bell


def column(row, rows):
    return jnp.transpose(jnp.broadcast_to(row, (128, rows)))


def kernel(
    v_hbm, w_hbm, mix_hbm, bias_hbm, head_hbm, hb_hbm, ow_hbm, cot_hbm, ez_hbm, ei_hbm, r_hbm, t1_hbm, t2_hbm,
    pred_out, field_out, spec_out, mixg_out, headg_out,
    v_in, w_in, mix_in, bias_in, head_in, hb_in, ow_in, cot_in, ez_in, ei_in, r_rows, t1_in, t2_in, r_in,
    vf, vy, wflat, wall, wst, wcat, mixed, hidden, gp, slope, gpre, fin, lhs, srow, arow, own,
    asend, arecv, bsend, brecv, crecv, dsend, drecv,
    g1send, g1recv, g2send, g2recv, g3recv,
    in_sem, send_sem, recv_sem, passed,
):
    w = lax.axis_index("wide")
    n = lax.axis_index("narrow")
    y, zl, c = w // 16, lax.rem(w // 2, 8), lax.rem(w, 2)
    x, zh = n // 2, lax.rem(n, 2)
    q = x * 8 + y * 2 + c
    z = zh * 8 + zl
    kind, block = lax.rem(zl, 4), 2 * zh + zl // 4

    cross = []
    for dx, dy, dc in CROSS:
        x2, y2, c2 = lax.rem(x + dx, 4), lax.rem(y + dy, 4), lax.rem(c + dc, 2)
        cross.append((x2, y2, c2, (y2 * 16 + zl * 2 + c2, x2 * 2 + zh)))
    ring = []
    for d in RING:
        z2 = lax.rem(z + d, 16)
        ring.append((z2, (y * 16 + lax.rem(z2, 8) * 2 + c, x * 2 + z2 // 8)))
    near = [ring[RING.index(d)][1] for d in (14, 1, 15)]
    alike = [ring[RING.index(d)][1] for d in (8, 4, 12)]
    up, down = lax.rem(z + 4, 16), lax.rem(z + 12, 16)
    up, down = 2 * (up // 8) + lax.rem(up, 8) // 4, 2 * (down // 8) + lax.rem(down, 8) // 4

    barrier = pltpu.get_barrier_semaphore()
    close = [where for d, (_, where) in zip(RING, ring) if min(d, 16 - d) <= 4]
    for where in close + [item[-1] for item in cross]:
        pl.semaphore_signal(barrier, inc=1, device_id=where, device_id_type=MESH)

    variant = y * 8 + zl
    loads = [
        (v_hbm, v_in), (ez_hbm, ez_in), (r_hbm.at[n], r_rows), (t1_hbm.at[variant], t1_in), (w_hbm, w_in),
        (mix_hbm, mix_in), (bias_hbm, bias_in), (head_hbm, head_in), (hb_hbm, hb_in), (ow_hbm, ow_in),
        (cot_hbm, cot_in), (ei_hbm, ei_in), (t2_hbm.at[variant], t2_in),
    ]
    loads = [pltpu.make_async_copy(a, b, in_sem.at[i]) for i, (a, b) in enumerate(loads)]
    for load in loads:
        load.start()

    def send(source, target, where, stage):
        pltpu.make_async_remote_copy(
            src_ref=source, dst_ref=target, send_sem=send_sem.at[stage], recv_sem=recv_sem.at[stage],
            device_id=where, device_id_type=MESH,
        ).start()

    def arrived(buffer, count, stage):
        part = buffer.at[pl.ds(0, count)]
        pltpu.make_async_copy(part, part, recv_sem.at[stage]).wait()

    def sent(buffer, count, stage):
        part = buffer.at[pl.ds(0, count)]
        pltpu.make_async_copy(part, part, send_sem.at[stage]).wait()

    def local_analysis(values, flag, turn):
        spectra = dot(ez_in[flag], values, (1, 1)).astype(BF)
        planes = dot(spectra[:32], r_in[:256], (1, 0)) + dot(spectra[32:], r_in[256:], (1, 0))
        for x2 in range(4):
            for c2 in range(2):
                first = planes[8 * x2 : 8 * x2 + 8, 256 * c2 : 256 * c2 + 128]
                second = planes[8 * x2 : 8 * x2 + 8, 256 * c2 + 128 : 256 * c2 + 256]
                asend[turn, x2 * 2 + c2] = jnp.concatenate([first, second], axis=0).astype(BF)
        arecv[turn, q] = asend[turn, x * 2 + c]

    def analysis_send(turn):
        for x2, y2, c2, where in cross:
            send(asend.at[turn, x2 * 2 + c2], arecv.at[turn, q], where, 4 * turn)

    def analysis_middle(turn):
        arrived(arecv.at[turn], 31, 4 * turn)
        table = t1_in[...]
        table = jnp.concatenate([table] * 4, axis=1)
        partial = dot(table, arecv[turn].reshape(512, 128), (1, 0)).astype(BF)
        for piece in range(4):
            bsend[turn, piece] = partial[16 * piece : 16 * piece + 16]
        brecv[turn, z] = bsend[turn, kind]
        for z2, where in ring:
            send(bsend.at[turn, lax.rem(z2, 4)], brecv.at[turn, z], where, 4 * turn + 1)

    def analysis_end(turn):
        arrived(brecv.at[turn], 15, 4 * turn + 1)
        total = brecv[turn, 0].astype(F32)
        for z2 in range(1, 16):
            total = total + brecv[turn, z2].astype(F32)
        for i in range(4):
            own[turn, i] = total[4 * i : 4 * i + 4]
        return total

    def paired(spectrum, low_sign, high_sign):
        for i in range(4):
            srow[4 * i : 4 * i + 2] = low_sign * spectrum[4 * i + 2 : 4 * i + 4]
            srow[4 * i + 2 : 4 * i + 4] = high_sign * spectrum[4 * i : 4 * i + 2]
        turned = srow[...]
        row = lax.broadcasted_iota(jnp.int32, (16, 128), 0)
        parts = []
        for i in range(4):
            for k2 in range(2):
                mine = (row // 4 == i) & (lax.rem(row, 2) == k2)
                parts += [jnp.where(mine, spectrum, 0.0), jnp.where(mine, turned, 0.0)]
        return jnp.concatenate(parts, axis=1).astype(BF)

    def synthesis_start(modes, turn):
        crecv[turn, kind] = modes.astype(BF)
        for where in near:
            send(crecv.at[turn, kind], crecv.at[turn, kind], where, 4 * turn + 2)

    def synthesis_middle(turn):
        arrived(crecv.at[turn], 3, 4 * turn + 2)
        planes = dot(t2_in[...], crecv[turn].reshape(64, 128), (0, 0)).astype(BF)
        for piece in range(8):
            dsend[turn, piece] = planes[16 * piece : 16 * piece + 16]
        drecv[turn, q] = dsend[turn, y * 2 + c]
        for x2, y2, c2, where in cross:
            send(dsend.at[turn, y2 * 2 + c2], drecv.at[turn, q], where, 4 * turn + 3)

    def synthesis_end(flag, turn):
        arrived(drecv.at[turn], 31, 4 * turn + 3)
        for x2 in range(4):
            for c2 in range(2):
                block = drecv[turn, x2 * 8 + c2].astype(F32)
                for y2 in range(1, 4):
                    block = block + drecv[turn, x2 * 8 + y2 * 2 + c2].astype(F32)
                lhs[8 * x2 : 8 * x2 + 8, 256 * c2 : 256 * c2 + 128] = block[:8]
                lhs[8 * x2 : 8 * x2 + 8, 256 * c2 + 128 : 256 * c2 + 256] = block[8:]
        lines = dot(lhs[...].astype(BF), r_in[...], (1, 1)).astype(BF)
        stacked = jnp.concatenate([lines[:, :256], lines[:, 256:]], axis=0)
        return dot(stacked, ei_in[flag], (0, 0))

    for i in (0, 1, 2):
        loads[i].wait()
    keep = lax.rem(lax.broadcasted_iota(jnp.int32, (32, 512), 1), 32) == lax.broadcasted_iota(jnp.int32, (32, 512), 0)
    for row in range(16):
        spread = jnp.broadcast_to(r_rows[row : row + 1], (32, 512))
        r_in[32 * row : 32 * row + 32] = jnp.where(keep, spread, 0.0).astype(BF)
    vf[...] = v_in[...].astype(F32)
    for row in range(8):
        vy[32 * row : 32 * row + 32] = vf[pl.ds(row, 32, stride=8), :].astype(BF)
    local_analysis(vy[...], 0, 0)

    for load in loads[3:]:
        load.wait()
    for j4 in range(4):
        for k2 in range(2):
            for r in range(2):
                base = 128 * (2 * k2 + r) + 32 * j4
                wflat[:, base : base + 32] = w_in[j4, k2, r]
    wall[block] = wflat[...].astype(BF)
    bias_col = column(bias_in[...], 32)
    for row in range(8):
        mixed[32 * row : 32 * row + 32] = dot(mix_in[...], vy[32 * row : 32 * row + 32], (0, 0)) + bias_col
    head_col = column(hb_in[...], 128)
    out_col = column(ow_in[...].astype(F32), 128)

    pl.semaphore_wait(barrier, len(cross) + len(close))
    for where in alike[1:]:
        pl.semaphore_signal(passed, inc=1, device_id=where, device_id_type=MESH)
    for where in alike[1:]:
        send(wall.at[block], wall.at[block], where, 11)
    analysis_send(0)
    pl.semaphore_wait(passed, 2)
    analysis_middle(0)
    arrived(wall, 2, 11)
    low, high = pl.ds(0, 16), pl.ds(16, 16)
    send(wall.at[up, low], wall.at[up, low], alike[2], 12)
    send(wall.at[down, high], wall.at[down, high], alike[1], 12)
    arrived(wall, 1, 12)
    inside = lax.broadcasted_iota(jnp.int32, (128, 128), 0) // 32 == lax.broadcasted_iota(jnp.int32, (128, 128), 1) // 32
    for i in range(4):
        for part in range(4):
            compact = wall[i, :, 128 * part : 128 * part + 128].astype(F32)
            full = jnp.where(inside, jnp.concatenate([compact] * 4, axis=0), 0.0).astype(BF)
            base = 128 * (4 * i + part)
            wst[base : base + 128] = full
            wcat[:, base : base + 128] = full
    modes = dot(paired(analysis_end(0), -1.0, 1.0), wst[...], (1, 0))
    synthesis_start(modes, 0)
    synthesis_middle(0)
    pre = synthesis_end(1, 0) + mixed[...]

    value, rate = gelu_parts(pre)
    hidden[...] = value.astype(BF)
    gp[...] = rate
    for first in range(0, 8, 2):
        group = range(first, first + 2)
        side = jnp.concatenate([hidden[32 * row : 32 * row + 32] for row in group], axis=1)
        head_pre = dot(head_in[...], side, (0, 0)) + jnp.concatenate([head_col] * 2, axis=1)
        value, rate = gelu_parts(head_pre)
        line = dot(ow_in[...], value.astype(BF), (1, 0))
        drive = jnp.concatenate([cot_in[row : row + 1] * out_col for row in group], axis=1)
        tilt = (drive * rate).astype(BF)
        back = dot(head_in[...], tilt, (1, 0))
        for i, row in enumerate(group):
            lanes = slice(128 * i, 128 * i + 128)
            pred_out[row : row + 1] = line[:, lanes]
            slope[128 * row : 128 * row + 128] = tilt[:, lanes]
            gpre[32 * row : 32 * row + 32] = (back[:, lanes] * gp[32 * row : 32 * row + 32]).astype(BF)
    local_analysis(gpre[...], 1, 1)
    analysis_send(1)

    head_grad = jnp.zeros((32, 128), F32)
    mix_grad = jnp.zeros((32, 32), F32)
    for row in range(8):
        head_grad = head_grad + dot(hidden[32 * row : 32 * row + 32], slope[128 * row : 128 * row + 128], (1, 1))
        mix_grad = mix_grad + dot(vy[32 * row : 32 * row + 32], gpre[32 * row : 32 * row + 32], (1, 1))
    folded = jnp.concatenate([mix_grad[8 * i : 8 * i + 8] for i in range(4)], axis=1)
    for i in range(16):
        g1send[i] = head_grad[2 * i : 2 * i + 2]
    for i in range(4):
        g1send[16 + i] = folded[2 * i : 2 * i + 2]
    for i in range(20, 32):
        g1send[i] = jnp.zeros((2, 128), F32)
    g1recv[q] = g1send[q]
    for x2, y2, c2, where in cross:
        send(g1send.at[x2 * 8 + y2 * 2 + c2], g1recv.at[q], where, 8)
    for row in range(8):
        mixed[32 * row : 32 * row + 32] = dot(mix_in[...], gpre[32 * row : 32 * row + 32], (1, 0))

    analysis_middle(1)

    arrived(g1recv, 31, 8)
    total = g1recv[0]
    for i in range(1, 32):
        total = total + g1recv[i]
    g2send[...] = total
    g2recv[z] = total
    for z2, where in ring:
        send(g2send, g2recv.at[z], where, 9)

    modes = dot(paired(analysis_end(1), 1.0, -1.0), wcat[...], (1, 1))
    synthesis_start(modes, 1)
    spectrum = own[0, block]
    adjoint = own[1, block]

    arrived(g2recv, 15, 9)
    total = g2recv[0]
    for i in range(1, 16):
        total = total + g2recv[i]
    g3recv[q] = total
    for x2, y2, c2, where in cross:
        send(g3recv.at[q], g3recv.at[q], where, 10)

    synthesis_middle(1)

    for j4 in range(4):
        arow[4 * j4 : 4 * j4 + 4] = adjoint[:, 32 * j4 : 32 * j4 + 32]
    rows = lax.broadcasted_iota(jnp.int32, (16, 128), 0)
    lanes = lax.broadcasted_iota(jnp.int32, (16, 128), 1)
    diagonal = rows // 4 == lanes // 32
    targets = arow[...].astype(BF)
    part = lax.rem(rows, 4)
    for k2 in range(2):
        real = jnp.broadcast_to(spectrum[k2 : k2 + 1], (16, 128))
        imag = jnp.broadcast_to(spectrum[2 + k2 : 3 + k2], (16, 128))
        for r in range(2):
            on_real = real if r == 0 else -imag
            on_imag = imag if r == 0 else real
            left = jnp.where(part == k2, on_real, jnp.where(part == 2 + k2, on_imag, 0.0))
            left = jnp.where(diagonal, left, 0.0).astype(BF)
            product = dot(left, targets, (0, 0))
            for j4 in range(4):
                spec_out[j4, k2, r] = product[32 * j4 : 32 * j4 + 32]

    arrived(g3recv, 31, 10)
    for i in range(16):
        headg_out[2 * i : 2 * i + 2] = g3recv[i]
    for i in range(4):
        rows2 = g3recv[16 + i]
        for j in range(4):
            mixg_out[8 * j + 2 * i : 8 * j + 2 * i + 2] = rows2[:, 32 * j : 32 * j + 32]

    field = synthesis_end(0, 1) + mixed[...]
    for row in range(8):
        fin[pl.ds(row, 32, stride=8), :] = field[32 * row : 32 * row + 32]
    field_out[...] = fin[...].astype(BF)

    for turn in range(2):
        sent(arecv.at[turn], 31, 4 * turn)
        sent(brecv.at[turn], 15, 4 * turn + 1)
        sent(crecv.at[turn], 3, 4 * turn + 2)
        sent(drecv.at[turn], 31, 4 * turn + 3)
    sent(g1recv, 31, 8)
    sent(g2recv, 15, 9)
    sent(g3recv, 31, 10)
    sent(wall, 2, 11)
    sent(wall, 1, 12)


def publish(*refs):
    sem = refs[-1]
    copies = [pltpu.make_async_copy(refs[i], refs[5 + i], sem.at[i]) for i in (2, 1, 0, 3, 4)]
    for copy in copies:
        copy.start()
    for copy in copies:
        copy.wait()


def body(lifted_field, spectral_weight, mix_weight, mix_bias, head_weight, head_bias, out_weight, cotangent):
    forward_z, inverse_z = z_tables()
    forward_x, inverse_x = x_tables()
    inputs = (
        lifted_field.reshape(256, 128), spectral_weight, mix_weight, mix_bias.reshape(1, 32), head_weight,
        head_bias.reshape(1, 128), out_weight.reshape(1, 128), cotangent.reshape(8, 128),
        jnp.asarray(forward_z), jnp.asarray(inverse_z), jnp.asarray(y_tables()), jnp.asarray(forward_x), jnp.asarray(inverse_x),
    )
    inputs = tuple(pltpu.with_memory_space_constraint(a, pltpu.HBM) for a in inputs)
    whole = lambda a: pltpu.VMEM(a.shape, a.dtype)
    tail = lambda a: pltpu.VMEM(a.shape[1:], a.dtype)
    outputs = [
        jax.ShapeDtypeStruct((8, 128), F32), jax.ShapeDtypeStruct((256, 128), BF),
        jax.ShapeDtypeStruct((4, 2, 2, 32, 32), F32), jax.ShapeDtypeStruct((32, 32), F32), jax.ShapeDtypeStruct((32, 128), F32),
    ]
    scratch = [whole(a) for a in inputs[:10]] + [tail(a) for a in inputs[10:]] + [pltpu.VMEM((512, 512), BF)]
    scratch += [
        pltpu.VMEM((256, 128), F32), pltpu.VMEM((256, 128), BF), pltpu.VMEM((32, 512), F32), pltpu.VMEM((4, 32, 512), BF),
        pltpu.VMEM((2048, 128), BF), pltpu.VMEM((128, 2048), BF),
        pltpu.VMEM((256, 128), F32), pltpu.VMEM((256, 128), BF), pltpu.VMEM((256, 128), F32), pltpu.VMEM((1024, 128), BF),
        pltpu.VMEM((256, 128), BF), pltpu.VMEM((256, 128), F32), pltpu.VMEM((32, 512), F32),
        pltpu.VMEM((16, 128), F32), pltpu.VMEM((16, 32), F32), pltpu.VMEM((2, 4, 4, 128), F32),
    ]
    scratch += [
        pltpu.VMEM((2, 8, 16, 128), BF), pltpu.VMEM((2, 32, 16, 128), BF),
        pltpu.VMEM((2, 4, 16, 128), BF), pltpu.VMEM((2, 16, 16, 128), BF), pltpu.VMEM((2, 4, 16, 128), BF),
        pltpu.VMEM((2, 8, 16, 128), BF), pltpu.VMEM((2, 32, 16, 128), BF),
        pltpu.VMEM((32, 2, 128), F32), pltpu.VMEM((32, 2, 128), F32),
        pltpu.VMEM((2, 128), F32), pltpu.VMEM((16, 2, 128), F32), pltpu.VMEM((32, 2, 128), F32),
        pltpu.SemaphoreType.DMA((13,)), pltpu.SemaphoreType.DMA((13,)), pltpu.SemaphoreType.DMA((13,)), pltpu.SemaphoreType.REGULAR,
    ]
    results = pl.pallas_call(
        kernel,
        out_shape=outputs,
        in_specs=[pl.BlockSpec(memory_space=pltpu.HBM)] * len(inputs),
        out_specs=[pl.BlockSpec(memory_space=pltpu.VMEM)] * len(outputs),
        scratch_shapes=scratch,
        name="step",
        compiler_params=pltpu.CompilerParams(collective_id=0, has_side_effects=True, vmem_limit_bytes=32 << 20),
    )(*inputs)
    prediction, field, spectral, mix_grad, head_grad = pl.pallas_call(
        publish,
        out_shape=outputs,
        in_specs=[pl.BlockSpec(memory_space=pltpu.VMEM)] * len(outputs),
        out_specs=[pl.BlockSpec(memory_space=pltpu.HBM)] * len(outputs),
        scratch_shapes=[pltpu.SemaphoreType.DMA((5,))],
        name="publish",
        compiler_params=pltpu.CompilerParams(vmem_limit_bytes=4 << 20),
    )(*results)
    return prediction.reshape(1, 8, 128), field.reshape(1, 32, 8, 128), spectral, mix_grad, head_grad


def solution(mesh):
    return jax.shard_map(
        body,
        mesh=mesh,
        in_specs=(
            P("wide", None, "narrow", None),
            P("wide", "narrow", None, None, None),
            P(),
            P(),
            P(),
            P(),
            P(),
            P("wide", "narrow", None),
        ),
        out_specs=(
            P("wide", "narrow", None),
            P("wide", None, "narrow", None),
            P("wide", "narrow", None, None, None),
            P(),
            P(),
        ),
        check_vma=False,
    )
```
